32 devices in a mesh: dp: 2 (over x), mp: 4 (over z), section: 4 (over y, core).
Axes of the slice: x: 2, y: 2, z: 4, core: 2. Of those that a mesh axis runs over, the one named last changes fastest.
Arguments:
- hidden: bfloat16 [512, 24576], P('dp', ('mp', 'section')), may hold values from -6 to 6
- fc_weight: bfloat16 [4096, 24576], P('dp', ('mp', 'section')), may hold values from -0.0390625 to 0.0390625
- gain_query: float32 [4096], P(('mp', 'section')), may hold values from 0.25 to 2.5
- gain_key: float32 [4096], P(('mp', 'section')), may hold values from 0.25 to 2.5
- block_mask: int32 [8, 4], P('dp'), may hold values 0 or 1
- cotangent: bfloat16 [2, 512, 4096], P(None, 'dp', ('mp', 'section')), may hold values from -6 to 6
Outputs:
- ttt_out: bfloat16 [2, 512, 4096], P(None, 'dp', ('mp', 'section'))
- fc_grad: float32 [4096, 24576], P('dp', ('mp', 'section'))
The draws below stay inside these ranges and needn't reach their ends.
All inputs are finite; a program needn't handle non-finite values. No bound on the sum of `block_mask` on one device may be relied on, other than what follows from the above.
Results may differ from the reference program's by a relative error of at most 0.015.
Values may be sent and summed in bfloat16 or wider, within the bound.
No kernel may reach another device: no remote copies, remote signals or barrier semaphores. Data moves between devices by JAX's collectives and lax.ppermute only.
A program may use at most 128 MiB of HBM per device.

```python
import math
from functools import partial
import jax
import jax.numpy as jnp
from jax import lax

JOIN_IN = 24576
HD = 128
WIN = 4096
SEQ = 256
NB = 4
TOKENS = 512
N_DP = 2


def draw_hidden(key, part):
    count = TOKENS // SEQ
    clusters = 8
    key_proto = jax.random.fold_in(key, 11)
    key_ids = jax.random.fold_in(key, 12)
    key_noise = jax.random.fold_in(key, 13)
    proto = jax.random.normal(key_proto, (count, clusters, JOIN_IN), jnp.float32)
    labels = jax.random.randint(key_ids, (count, SEQ), 0, clusters)
    noise = 0.55 * jax.random.normal(key_noise, (count, SEQ, JOIN_IN), jnp.float32)
    chosen = jax.vmap(lambda table, picks: table[picks])(proto, labels)
    values = jnp.clip(chosen + noise, -6.0, 6.0)
    return values.reshape(TOKENS, JOIN_IN).astype(jnp.bfloat16)


def touch_ends(values, key, low, top_value):
    shape = values.shape
    place = [jax.random.randint(jax.random.fold_in(key, axis), (), 0, shape[axis]) for axis in range(len(shape))]
    values = values.at[tuple(place)].set(low)
    longest = shape.index(max(shape))
    place[longest] = (place[longest] + 1) % shape[longest]
    return values.at[tuple(place)].set(top_value)


def with_spikes(entries, stream_key, source, target, parts, factor):
    owner, partner = [(jnp.arange(entries.shape[dim]) // (entries.shape[dim] // parts)).reshape([-1 if axis == dim else 1 for axis in range(entries.ndim)]) for dim in (source, target)]
    chosen = jax.random.permutation(stream_key, parts)[partner]
    strong = (owner == chosen) | (owner == (partner + parts // 2) % parts)
    return jnp.where(strong, factor * entries, entries)


def shard_levels(stream_key, extent, pieces, least, high):
    level = 1.0
    for dim, blocks in pieces:
        draws = jax.random.uniform(jax.random.fold_in(jax.random.fold_in(stream_key, 6), dim), (blocks,), jnp.float32, least / len(pieces), high / len(pieces))
        level = level * jnp.repeat(jnp.exp(draws), extent[dim] // blocks).reshape((-1,) + (1,) * (len(extent) - 1 - dim))
    return level


def normal_values(stream_key, dims, scale, limit, cuts=(), kind=jnp.bfloat16):
    result = jax.random.normal(stream_key, dims, jnp.float32) * scale
    if len(cuts) > 0:
        result = shard_levels(stream_key, dims, cuts, -0.22, 0.18) * result
    return jnp.clip(result, min=-limit, max=limit).astype(kind)


def bell_draw_with(key, dims, scale, bound, cuts, heavy, kind=jnp.bfloat16):
    array = scale * jax.random.normal(key, dims, jnp.float32)
    if cuts:
        array = array * shard_levels(key, dims, cuts, -0.22, 0.18)
    return jnp.clip(with_spikes(array, jax.random.fold_in(key, 3), *heavy), -bound, bound).astype(kind)


def setup_inputs(seed: int = 0) -> dict:
    splits = jax.random.split(jax.random.key(seed), 7)
    return {
        "hidden": draw_hidden(jax.random.fold_in(splits[6], 71), 0),
        "fc_weight": normal_values(splits[1], (WIN, JOIN_IN), JOIN_IN ** -0.5, 0.0390625, ((0, 2), (1, 16))),
        "gain_query": jnp.clip(jnp.exp(math.log(2.5) - 2.3025851 * jax.random.uniform(splits[2], (WIN,), jnp.float32) ** shard_levels(splits[2], (WIN,), ((0, 16),), -0.2, 0.2)), 0.25, 2.5),
        "gain_key": jnp.clip(jnp.exp(math.log(2.5) - 2.3025851 * jax.random.uniform(splits[3], (WIN,), jnp.float32) ** shard_levels(splits[3], (WIN,), ((0, 16),), -0.2, 0.2)), 0.25, 2.5),
        "block_mask": touch_ends((jax.random.randint(splits[4], (N_DP * NB, NB), 0, 2) < 1).astype(jnp.int32), jax.random.fold_in(splits[4], 1), 0, 1),
        "cotangent": bell_draw_with(splits[5], (2, TOKENS, WIN), 1.0, 6.0, ((1, 2), (2, 16)), (1, 2, 16, 2.0)),
    }


EPS = 1e-06

def rms_scale(values):
    return values * lax.rsqrt(lax.optimization_barrier(jnp.mean(values * values, axis=-1, keepdims=True)) + EPS)

def visible_sets(block_mask, length):
    position = jnp.arange(length, dtype=jnp.int32)
    block_of = position // 64
    onehot = (block_of[:, None] == jnp.arange(block_mask.shape[0], dtype=jnp.int32)[None, :]).astype(jnp.float32)
    opened = jnp.dot(jnp.dot(onehot, block_mask.astype(jnp.float32), precision=lax.Precision.HIGHEST), onehot.T, precision=lax.Precision.HIGHEST) > 0.5
    earlier = block_of[None, :] < block_of[:, None]
    same_block = block_of[None, :] == block_of[:, None]
    causal = position[None, :] <= position[:, None]
    first = causal & (same_block | opened & earlier)
    second = first & (position[None, :] < position[:, None])
    return (first, second)

def head_steps(joined_head, gain_query, gain_key, first, second):
    scale = joined_head.shape[-1] ** (-0.5)
    normed = rms_scale(joined_head.astype(jnp.float32))
    queries = normed * gain_query
    keys_ctx = normed * gain_key
    scores = jnp.dot(queries, keys_ctx.T, precision=lax.Precision.HIGHEST) * scale
    scores = jnp.where(first, scores, -jnp.inf)
    top_one = lax.optimization_barrier(jnp.max(scores, axis=-1, keepdims=True))
    expo_one = jnp.exp(scores - top_one)
    weights_one = (expo_one / lax.optimization_barrier(jnp.sum(expo_one, axis=-1, keepdims=True))).astype(jnp.bfloat16)
    step_one = jnp.dot(weights_one, joined_head, preferred_element_type=jnp.float32).astype(jnp.bfloat16)
    renorm = rms_scale(step_one.astype(jnp.float32))
    queries_two = renorm * gain_query
    own_key = renorm * gain_key
    scores_two = jnp.dot(queries_two, keys_ctx.T, precision=lax.Precision.HIGHEST) * scale
    scores_two = jnp.where(second, scores_two, -jnp.inf)
    own_score = lax.optimization_barrier(jnp.sum(queries_two * own_key, axis=-1)) * scale
    top_two = jnp.maximum(lax.optimization_barrier(jnp.max(scores_two, axis=-1)), own_score)
    expo_two = jnp.exp(scores_two - top_two[:, None])
    own_expo = jnp.exp(own_score - top_two)
    total = lax.optimization_barrier(jnp.sum(expo_two, axis=-1)) + own_expo
    weights_two = (expo_two / total[:, None]).astype(jnp.bfloat16)
    step_two = jnp.dot(weights_two, joined_head, preferred_element_type=jnp.float32) + (own_expo / total)[:, None] * step_one.astype(jnp.float32)
    return (step_one, step_two.astype(jnp.bfloat16))

def sequence_steps(joined_seq, gain_query, gain_key, block_mask):
    length, width = joined_seq.shape
    heads = width // HD
    first, second = visible_sets(block_mask, length)
    split = joined_seq.reshape(length, heads, HD).transpose(1, 0, 2)
    one_out, two_out = jax.vmap(head_steps, in_axes=(0, 0, 0, None, None))(split, gain_query.reshape(heads, HD), gain_key.reshape(heads, HD), first, second)
    return (one_out.transpose(1, 0, 2).reshape(length, width), two_out.transpose(1, 0, 2).reshape(length, width))

def sequence_train(joined_seq, gain_query, gain_key, block_mask, cot_one, cot_two):
    forward = partial(sequence_steps, gain_query=gain_query, gain_key=gain_key, block_mask=block_mask)
    outputs, pullback = jax.vjp(forward, joined_seq)
    grads = pullback((cot_one, cot_two))
    return (outputs[0], outputs[1], grads[0])

def reference(hidden, fc_weight, gain_query, gain_key, block_mask, cotangent):
    joined = jnp.dot(hidden, fc_weight.T, preferred_element_type=jnp.float32).astype(jnp.bfloat16)
    joined_seqs = joined.reshape(N_DP, SEQ, WIN)
    masks = block_mask.reshape(N_DP, NB, NB)
    cot_seqs = cotangent.reshape(2, N_DP, SEQ, WIN)

    def one_sequence(items):
        return sequence_train(items[0], gain_query, gain_key, items[1], items[2], items[3])
    step_one, step_two, d_joined = lax.map(one_sequence, (joined_seqs, masks, cot_seqs[0], cot_seqs[1]))
    hidden_seqs = hidden.reshape(N_DP, SEQ, JOIN_IN)

    def accumulate(total, items):
        term = lax.dot_general(items[0], items[1], (((0,), (0,)), ((), ())), preferred_element_type=jnp.float32)
        return (total + term, None)
    fc_grad, unused = lax.scan(accumulate, jnp.zeros((WIN, JOIN_IN), jnp.float32), (d_joined, hidden_seqs))
    ttt_out = jnp.stack([step_one.reshape(TOKENS, WIN), step_two.reshape(TOKENS, WIN)])
    return (ttt_out, fc_grad)
```

```python
from functools import partial

import jax
import jax.numpy as jnp
from jax import lax
from jax.experimental import pallas as pl
from jax.experimental.pallas import tpu as pltpu
from jax.sharding import PartitionSpec as P

HD = 128


EPS = 1e-06


def rms_scale(values):
    return values * lax.rsqrt(jnp.mean(values * values, axis=-1, keepdims=True) + EPS)


def visible_sets(block_mask, length):
    position = jnp.arange(length, dtype=jnp.int32)
    block_of = position // 64
    onehot = (
        block_of[:, None] == jnp.arange(block_mask.shape[0], dtype=jnp.int32)[None, :]
    ).astype(jnp.float32)
    opened = (
        jnp.dot(
            jnp.dot(onehot, block_mask.astype(jnp.float32), precision=lax.Precision.HIGHEST),
            onehot.T,
            precision=lax.Precision.HIGHEST,
        )
        > 0.5
    )
    earlier = block_of[None, :] < block_of[:, None]
    same_block = block_of[None, :] == block_of[:, None]
    causal = position[None, :] <= position[:, None]
    first = causal & (same_block | opened & earlier)
    second = first & (position[None, :] < position[:, None])
    return (first, second)


def head_steps(joined_head, gain_query, gain_key, first, second):
    scale = joined_head.shape[-1] ** (-0.5)
    normed = rms_scale(joined_head.astype(jnp.float32))
    queries = normed * gain_query
    keys_ctx = normed * gain_key
    scores = jnp.dot(queries, keys_ctx.T, precision=lax.Precision.HIGHEST) * scale
    scores = jnp.where(first, scores, -jnp.inf)
    top_one = jnp.max(scores, axis=-1, keepdims=True)
    expo_one = jnp.exp(scores - top_one)
    weights_one = (expo_one / jnp.sum(expo_one, axis=-1, keepdims=True)).astype(jnp.bfloat16)
    step_one = jnp.dot(weights_one, joined_head, preferred_element_type=jnp.float32).astype(
        jnp.bfloat16
    )
    renorm = rms_scale(step_one.astype(jnp.float32))
    queries_two = renorm * gain_query
    own_key = renorm * gain_key
    scores_two = jnp.dot(queries_two, keys_ctx.T, precision=lax.Precision.HIGHEST) * scale
    scores_two = jnp.where(second, scores_two, -jnp.inf)
    own_score = jnp.sum(queries_two * own_key, axis=-1) * scale
    top_two = jnp.maximum(jnp.max(scores_two, axis=-1), own_score)
    expo_two = jnp.exp(scores_two - top_two[:, None])
    own_expo = jnp.exp(own_score - top_two)
    total = jnp.sum(expo_two, axis=-1) + own_expo
    weights_two = (expo_two / total[:, None]).astype(jnp.bfloat16)
    step_two = jnp.dot(weights_two, joined_head, preferred_element_type=jnp.float32) + (
        own_expo / total
    )[:, None] * step_one.astype(jnp.float32)
    return (step_one, step_two.astype(jnp.bfloat16))


def sequence_steps(joined_seq, gain_query, gain_key, block_mask):
    length, width = joined_seq.shape
    heads = width // HD
    first, second = visible_sets(block_mask, length)
    split = joined_seq.reshape(length, heads, HD).transpose(1, 0, 2)
    one_out, two_out = jax.vmap(head_steps, in_axes=(0, 0, 0, None, None))(
        split, gain_query.reshape(heads, HD), gain_key.reshape(heads, HD), first, second
    )
    return (
        one_out.transpose(1, 0, 2).reshape(length, width),
        two_out.transpose(1, 0, 2).reshape(length, width),
    )


def sequence_train(joined_seq, gain_query, gain_key, block_mask, cot_one, cot_two):
    forward = partial(
        sequence_steps, gain_query=gain_query, gain_key=gain_key, block_mask=block_mask
    )
    outputs, pullback = jax.vjp(forward, joined_seq)
    grads = pullback((cot_one, cot_two))
    return (outputs[0], outputs[1], grads[0])


def gather_weights_plan(hidden, fc_weight, gain_query, gain_key, block_mask, cotangent):
    partial_joined = lax.dot_general(
        hidden,
        lax.all_gather(fc_weight, "dp", axis=0, tiled=True),
        (((1,), (1,)), ((), ())),
        preferred_element_type=jnp.float32,
    )
    joined = lax.psum_scatter(
        partial_joined, ("mp", "section"), scatter_dimension=1, tiled=True
    ).astype(jnp.bfloat16)
    step_one, step_two, d_joined = sequence_train(
        joined, gain_query, gain_key, block_mask, cotangent[0], cotangent[1]
    )
    ttt_out = jnp.stack([step_one, step_two])
    grad_full = lax.all_gather(d_joined, ("mp", "section"), axis=1, tiled=True)
    fc_grad = lax.psum_scatter(
        lax.dot_general(
            grad_full, hidden, (((0,), (0,)), ((), ())), preferred_element_type=jnp.float32
        ),
        "dp",
        scatter_dimension=0,
        tiled=True,
    )
    return (ttt_out, fc_grad)


def take(array, index):
    return lax.dynamic_index_in_dim(array, index, 0, keepdims=False)


def swap(axis, size, bit):
    return lambda array: lax.ppermute(array, axis, [(i, i ^ bit) for i in range(size)])


def half_product_kernel(core_ref, hidden_ref, weight_ref, out_ref, rows, sems):
    core = core_ref[0]
    copies = []
    for y in range(2):
        for z0 in range(2):
            block = 4 * z0 + 2 * y + core
            copy = pltpu.make_async_copy(
                weight_ref.at[pl.ds(block * 2 * HD, 2 * HD)], rows.at[2 * y + z0], sems.at[2 * y + z0]
            )
            copy.start()
            copies.append(copy)
    for y in range(2):
        for z0 in range(2):
            copies[2 * y + z0].wait()
            product = lax.dot_general(
                hidden_ref[...],
                rows[2 * y + z0],
                (((1,), (1,)), ((), ())),
                preferred_element_type=jnp.float32,
            )
            out_ref[y, z0] = product[:, :HD].astype(out_ref.dtype)
            out_ref[y, 2 + z0] = product[:, HD:].astype(out_ref.dtype)


def half_product(hidden, weight, core, dtype):
    tokens, features = hidden.shape
    vmem = pl.BlockSpec(memory_space=pltpu.VMEM)
    return pl.pallas_call(
        half_product_kernel,
        grid_spec=pltpu.PrefetchScalarGridSpec(
            num_scalar_prefetch=1,
            grid=(),
            in_specs=[vmem, pl.BlockSpec(memory_space=pl.ANY)],
            out_specs=vmem,
            scratch_shapes=[
                pltpu.VMEM((4, 2 * HD, features), weight.dtype),
                pltpu.SemaphoreType.DMA((4,)),
            ],
        ),
        out_shape=jax.ShapeDtypeStruct((2, 4, tokens, HD), dtype),
        compiler_params=pltpu.CompilerParams(vmem_limit_bytes=24 << 20),
        cost_estimate=pl.CostEstimate(
            flops=2 * tokens * features * 8 * HD,
            bytes_accessed=2 * features * 8 * HD + 2 * tokens * features,
            transcendentals=0,
        ),
    )(core.reshape(1), hidden, weight)


def grad_kernel(table_ref, own_ref, other_ref, hidden_ref, hidden_other_ref, *rest):
    out_ref, total, sems = rest[-3:]
    groups = own_ref.shape[0] // 4
    copies = []
    for g in range(groups):
        left = jnp.concatenate([own_ref[4 * g + i] for i in range(4)], axis=0)
        right = jnp.concatenate([other_ref[4 * g + i] for i in range(4)], axis=0)
        total[g] = jnp.dot(left, hidden_ref[...], preferred_element_type=jnp.float32) + jnp.dot(
            right, hidden_other_ref[...], preferred_element_type=jnp.float32
        )
        for i in range(4):
            row = pl.multiple_of(table_ref[4 * g + i] * HD, HD)
            copy = pltpu.make_async_copy(
                total.at[g, pl.ds(i * HD, HD)], out_ref.at[pl.ds(row, HD)], sems.at[4 * g + i]
            )
            copy.start()
            copies.append(copy)
    for copy in copies:
        copy.wait()


def grad_rows(table, own, other, hidden, hidden_other, rows, previous=None):
    heads = own.shape[0]
    tokens, features = hidden.shape
    vmem = pl.BlockSpec(memory_space=pltpu.VMEM)
    hbm = pl.BlockSpec(memory_space=pl.ANY)
    args = [table, own, other, hidden, hidden_other] + ([] if previous is None else [previous])
    return pl.pallas_call(
        grad_kernel,
        grid_spec=pltpu.PrefetchScalarGridSpec(
            num_scalar_prefetch=1,
            grid=(),
            in_specs=[vmem] * 4 + ([] if previous is None else [hbm]),
            out_specs=hbm,
            scratch_shapes=[
                pltpu.VMEM((heads // 4, 4 * HD, features), jnp.float32),
                pltpu.SemaphoreType.DMA((heads,)),
            ],
        ),
        out_shape=jax.ShapeDtypeStruct((rows, features), jnp.float32),
        input_output_aliases={} if previous is None else {5: 0},
        compiler_params=pltpu.CompilerParams(vmem_limit_bytes=32 << 20),
        cost_estimate=pl.CostEstimate(
            flops=4 * heads * HD * tokens * features,
            bytes_accessed=4 * heads * HD * features,
            transcendentals=0,
        ),
    )(*args)


def head_train(joined, gain_query, gain_key, block_mask, cot_one, cot_two):
    first, second = visible_sets(block_mask, joined.shape[0])
    outputs, pullback = jax.vjp(
        lambda j: head_steps(j, gain_query, gain_key, first, second), joined
    )
    return outputs[0], outputs[1], pullback((cot_one, cot_two))[0]


def keep_weights_plan(hidden, fc_weight, gain_query, gain_key, block_mask, cotangent):
    me_dp = lax.axis_index("dp")
    me_z = lax.axis_index("mp")
    me_y = lax.axis_index("section") // 2
    me_c = lax.axis_index("section") % 2
    upper = me_z // 2
    over_x = swap("dp", 2, 1)
    over_y = swap("section", 4, 2)
    over_c = swap("section", 4, 1)
    over_z = [swap("mp", 4, bit) for bit in range(4)]

    def route(r):
        return [
            (4 * d + 2 * e + b, 4 * e + 2 * (d ^ r) + b)
            for d in range(2)
            for e in range(2)
            for b in range(2)
        ]

    hidden_other = over_x(hidden)
    tokens = hidden.shape[0]
    cot_heads = cotangent.reshape(2, tokens, 2, HD)
    cot_in = []
    for r in range(2):
        head = me_dp ^ r
        sent = lax.dynamic_index_in_dim(cot_heads, head, 2, keepdims=False)
        cot_in.append(lax.ppermute(sent, ("dp", "mp"), route(r)))
    gains = jnp.stack([gain_query, gain_key]).reshape(2, 2, HD)
    gains = lax.ppermute(
        lax.dynamic_index_in_dim(gains, me_dp, 1, keepdims=False), ("dp", "mp"), route(0)
    )
    mask_other = over_x(block_mask)
    own_first = upper == me_dp
    cot_own = jnp.where(own_first, cot_in[0], cot_in[1])
    cot_other = jnp.where(own_first, cot_in[1], cot_in[0])

    def scatter_sum(tokens_in):
        sent = half_product(tokens_in, fc_weight, 1 - me_c, jnp.bfloat16)
        kept = half_product(tokens_in, fc_weight, me_c, jnp.float32)
        got = over_c(sent)
        sums = kept + got.astype(jnp.float32)
        got = over_y(take(sums, 1 - me_y).astype(jnp.bfloat16))
        sums = take(sums, me_y) + got.astype(jnp.float32)
        pieces = [over_z[b](take(sums, me_z ^ b).astype(jnp.bfloat16)) for b in (1, 2, 3)]
        total = take(sums, me_z)
        for piece in pieces:
            total = total + piece.astype(jnp.float32)
        return total.astype(jnp.bfloat16)

    def spread(piece):
        part = jnp.stack([piece] + [over_z[b](piece) for b in (1, 2, 3)])
        near = jnp.concatenate([part, over_y(part)])
        return near, over_c(near)

    joined_own = scatter_sum(hidden)
    joined_other = scatter_sum(hidden_other)
    one_own, two_own, d_own = head_train(
        joined_own, gains[0], gains[1], block_mask, cot_own[0], cot_own[1]
    )
    near_own, far_own = spread(d_own.T)
    one_other, two_other, d_other = head_train(
        joined_other, gains[0], gains[1], mask_other, cot_other[0], cot_other[1]
    )
    near_other, far_other = spread(d_other.T)

    def table(core):
        ys = jnp.arange(2)[:, None]
        zs = jnp.arange(4)[None, :]
        z = me_z ^ zs
        y = me_y ^ ys
        return (2 * (4 * (z % 2) + 2 * y + core) + z // 2).reshape(8).astype(jnp.int32)

    rows = fc_weight.shape[0]
    fc_grad = grad_rows(table(me_c), near_own, near_other, hidden, hidden_other, rows)
    fc_grad = grad_rows(
        table(1 - me_c), far_own, far_other, hidden, hidden_other, rows, fc_grad
    )
    out_own = jnp.stack([one_own, two_own])
    out_other = jnp.stack([one_other, two_other])
    heads_back = []
    for r in range(2):
        back = [(b, a) for a, b in route(r)]
        sent = jnp.where((upper ^ r) == me_dp, out_own, out_other)
        heads_back.append(lax.ppermute(sent, ("dp", "mp"), back))
    low = jnp.where(me_dp == 0, heads_back[0], heads_back[1])
    high = jnp.where(me_dp == 0, heads_back[1], heads_back[0])
    ttt_out = jnp.concatenate([low, high], axis=2)
    return (ttt_out, fc_grad)


def per_device(sizes, hidden, fc_weight, *rest):
    heads = fc_weight.shape[0] // HD
    if sizes == (2, 4, 4) and heads == 16 and rest[0].shape[0] == 2 * HD:
        return keep_weights_plan(hidden, fc_weight, *rest)
    return gather_weights_plan(hidden, fc_weight, *rest)


def solution(mesh):
    in_specs = (
        P("dp", ("mp", "section")),
        P("dp", ("mp", "section")),
        P(("mp", "section")),
        P(("mp", "section")),
        P("dp", None),
        P(None, "dp", ("mp", "section")),
    )
    out_specs = (P(None, "dp", ("mp", "section")), P("dp", ("mp", "section")))
    sizes = tuple(mesh.shape[name] for name in ("dp", "mp", "section"))
    return jax.shard_map(
        partial(per_device, sizes), mesh=mesh, in_specs=in_specs, out_specs=out_specs, check_vma=False
    )
```

```python
from functools import partial

import jax
import jax.numpy as jnp
from jax import lax
from jax.experimental import pallas as pl
from jax.experimental.pallas import tpu as pltpu
from jax.sharding import PartitionSpec as P

HD = 128


EPS = 1e-06


def rms_scale(values):
    return values * lax.rsqrt(jnp.mean(values * values, axis=-1, keepdims=True) + EPS)


def visible_sets(block_mask, length):
    position = jnp.arange(length, dtype=jnp.int32)
    block_of = position // 64
    onehot = (
        block_of[:, None] == jnp.arange(block_mask.shape[0], dtype=jnp.int32)[None, :]
    ).astype(jnp.float32)
    opened = (
        jnp.dot(
            jnp.dot(onehot, block_mask.astype(jnp.float32), precision=lax.Precision.HIGHEST),
            onehot.T,
            precision=lax.Precision.HIGHEST,
        )
        > 0.5
    )
    earlier = block_of[None, :] < block_of[:, None]
    same_block = block_of[None, :] == block_of[:, None]
    causal = position[None, :] <= position[:, None]
    first = causal & (same_block | opened & earlier)
    second = first & (position[None, :] < position[:, None])
    return (first, second)


def head_steps(joined_head, gain_query, gain_key, first, second):
    scale = joined_head.shape[-1] ** (-0.5)
    normed = rms_scale(joined_head.astype(jnp.float32))
    queries = normed * gain_query
    keys_ctx = normed * gain_key
    scores = jnp.dot(queries, keys_ctx.T, precision=lax.Precision.HIGHEST) * scale
    scores = jnp.where(first, scores, -jnp.inf)
    top_one = jnp.max(scores, axis=-1, keepdims=True)
    expo_one = jnp.exp(scores - top_one)
    weights_one = (expo_one / jnp.sum(expo_one, axis=-1, keepdims=True)).astype(jnp.bfloat16)
    step_one = jnp.dot(weights_one, joined_head, preferred_element_type=jnp.float32).astype(
        jnp.bfloat16
    )
    renorm = rms_scale(step_one.astype(jnp.float32))
    queries_two = renorm * gain_query
    own_key = renorm * gain_key
    scores_two = jnp.dot(queries_two, keys_ctx.T, precision=lax.Precision.HIGHEST) * scale
    scores_two = jnp.where(second, scores_two, -jnp.inf)
    own_score = jnp.sum(queries_two * own_key, axis=-1) * scale
    top_two = jnp.maximum(jnp.max(scores_two, axis=-1), own_score)
    expo_two = jnp.exp(scores_two - top_two[:, None])
    own_expo = jnp.exp(own_score - top_two)
    total = jnp.sum(expo_two, axis=-1) + own_expo
    weights_two = (expo_two / total[:, None]).astype(jnp.bfloat16)
    step_two = jnp.dot(weights_two, joined_head, preferred_element_type=jnp.float32) + (
        own_expo / total
    )[:, None] * step_one.astype(jnp.float32)
    return (step_one, step_two.astype(jnp.bfloat16))


def sequence_steps(joined_seq, gain_query, gain_key, block_mask):
    length, width = joined_seq.shape
    heads = width // HD
    first, second = visible_sets(block_mask, length)
    split = joined_seq.reshape(length, heads, HD).transpose(1, 0, 2)
    one_out, two_out = jax.vmap(head_steps, in_axes=(0, 0, 0, None, None))(
        split, gain_query.reshape(heads, HD), gain_key.reshape(heads, HD), first, second
    )
    return (
        one_out.transpose(1, 0, 2).reshape(length, width),
        two_out.transpose(1, 0, 2).reshape(length, width),
    )


def sequence_train(joined_seq, gain_query, gain_key, block_mask, cot_one, cot_two):
    forward = partial(
        sequence_steps, gain_query=gain_query, gain_key=gain_key, block_mask=block_mask
    )
    outputs, pullback = jax.vjp(forward, joined_seq)
    grads = pullback((cot_one, cot_two))
    return (outputs[0], outputs[1], grads[0])


def gather_weights_plan(hidden, fc_weight, gain_query, gain_key, block_mask, cotangent):
    partial_joined = lax.dot_general(
        hidden,
        lax.all_gather(fc_weight, "dp", axis=0, tiled=True),
        (((1,), (1,)), ((), ())),
        preferred_element_type=jnp.float32,
    )
    joined = lax.psum_scatter(
        partial_joined, ("mp", "section"), scatter_dimension=1, tiled=True
    ).astype(jnp.bfloat16)
    step_one, step_two, d_joined = sequence_train(
        joined, gain_query, gain_key, block_mask, cotangent[0], cotangent[1]
    )
    ttt_out = jnp.stack([step_one, step_two])
    grad_full = lax.all_gather(d_joined, ("mp", "section"), axis=1, tiled=True)
    fc_grad = lax.psum_scatter(
        lax.dot_general(
            grad_full, hidden, (((0,), (0,)), ((), ())), preferred_element_type=jnp.float32
        ),
        "dp",
        scatter_dimension=0,
        tiled=True,
    )
    return (ttt_out, fc_grad)


def take(array, index):
    return lax.dynamic_index_in_dim(array, index, 0, keepdims=False)


def swap(axis, size, bit):
    return lambda array: lax.ppermute(array, axis, [(i, i ^ bit) for i in range(size)])


def half_product_kernel(core_ref, hidden_ref, weight_ref, out_ref, rows, sems):
    core = core_ref[0]
    copies = []
    for y in range(2):
        for z0 in range(2):
            block = 4 * z0 + 2 * y + core
            copy = pltpu.make_async_copy(
                weight_ref.at[pl.ds(block * 2 * HD, 2 * HD)], rows.at[2 * y + z0], sems.at[2 * y + z0]
            )
            copy.start()
            copies.append(copy)
    for y in range(2):
        for z0 in range(2):
            copies[2 * y + z0].wait()
            product = lax.dot_general(
                hidden_ref[...],
                rows[2 * y + z0],
                (((1,), (1,)), ((), ())),
                preferred_element_type=jnp.float32,
            )
            out_ref[y, z0] = product[:, :HD].astype(out_ref.dtype)
            out_ref[y, 2 + z0] = product[:, HD:].astype(out_ref.dtype)


def half_product(hidden, weight, core, dtype):
    tokens, features = hidden.shape
    vmem = pl.BlockSpec(memory_space=pltpu.VMEM)
    return pl.pallas_call(
        half_product_kernel,
        grid_spec=pltpu.PrefetchScalarGridSpec(
            num_scalar_prefetch=1,
            grid=(),
            in_specs=[vmem, pl.BlockSpec(memory_space=pltpu.HBM)],
            out_specs=vmem,
            scratch_shapes=[
                pltpu.VMEM((4, 2 * HD, features), weight.dtype),
                pltpu.SemaphoreType.DMA((4,)),
            ],
        ),
        out_shape=jax.ShapeDtypeStruct((2, 4, tokens, HD), dtype),
        compiler_params=pltpu.CompilerParams(vmem_limit_bytes=24 << 20),
        cost_estimate=pl.CostEstimate(
            flops=2 * tokens * features * 8 * HD,
            bytes_accessed=2 * features * 8 * HD + 2 * tokens * features,
            transcendentals=0,
        ),
    )(core.reshape(1), hidden, weight)


def grad_kernel(table_ref, *refs):
    pieces, (hidden_ref, hidden_other_ref), rest = refs[:4], refs[4:6], refs[6:]
    out_ref, total, sems = rest[-3:]
    copies = []
    for g in range(2):
        left = jnp.concatenate([pieces[g][i] for i in range(4)], axis=0)
        right = jnp.concatenate([pieces[2 + g][i] for i in range(4)], axis=0)
        total[g] = jnp.dot(left, hidden_ref[...], preferred_element_type=jnp.float32) + jnp.dot(
            right, hidden_other_ref[...], preferred_element_type=jnp.float32
        )
        for i in range(4):
            row = pl.multiple_of(table_ref[4 * g + i] * HD, HD)
            copy = pltpu.make_async_copy(
                total.at[g, pl.ds(i * HD, HD)], out_ref.at[pl.ds(row, HD)], sems.at[4 * g + i]
            )
            copy.start()
            copies.append(copy)
    for copy in copies:
        copy.wait()


def grad_rows(table, own, other, hidden, hidden_other, rows, previous=None):
    tokens, features = hidden.shape
    vmem = pl.BlockSpec(memory_space=pltpu.VMEM)
    hbm = pl.BlockSpec(memory_space=pltpu.HBM)
    before = [] if previous is None else [previous]
    return pl.pallas_call(
        grad_kernel,
        grid_spec=pltpu.PrefetchScalarGridSpec(
            num_scalar_prefetch=1,
            grid=(),
            in_specs=[vmem] * 6 + [hbm] * len(before),
            out_specs=hbm,
            scratch_shapes=[
                pltpu.VMEM((2, 4 * HD, features), jnp.float32),
                pltpu.SemaphoreType.DMA((8,)),
            ],
        ),
        out_shape=jax.ShapeDtypeStruct((rows, features), jnp.float32),
        input_output_aliases={7: 0} if before else {},
        compiler_params=pltpu.CompilerParams(vmem_limit_bytes=32 << 20),
        cost_estimate=pl.CostEstimate(
            flops=32 * HD * tokens * features,
            bytes_accessed=32 * HD * features,
            transcendentals=0,
        ),
    )(table, *own, *other, hidden, hidden_other, *before)


def pack_kernel(dp_ref, cot_ref, query_ref, key_ref, mask_ref, first_ref, second_ref):
    tokens = cot_ref.shape[1]
    for r, out_ref in enumerate((first_ref, second_ref)):
        lanes = pl.ds(pl.multiple_of((dp_ref[0] ^ r) * HD, HD), HD)
        out_ref[:tokens] = cot_ref[0, :, lanes]
        out_ref[tokens : 2 * tokens] = cot_ref[1, :, lanes]
        terms = []
        for gain_ref in (query_ref, key_ref):
            rest = gain_ref[:, lanes]
            for _ in range(3):
                term = rest.astype(jnp.bfloat16).astype(jnp.float32)
                terms.append(term)
                rest = rest - term
        terms.append(jnp.zeros((10, HD), jnp.float32))
        out_ref[2 * tokens : 2 * tokens + 16] = jnp.concatenate(terms, axis=0).astype(jnp.bfloat16)
        out_ref[2 * tokens + 16 :] = mask_ref[...].astype(jnp.bfloat16)


def pack(dp, cotangent, gain_query, gain_key, block_mask):
    tokens = cotangent.shape[1]
    blocks = block_mask.shape[0]
    mask = jnp.pad(block_mask.astype(jnp.float32), ((0, 16 - blocks), (0, HD - blocks)))
    vmem = pl.BlockSpec(memory_space=pltpu.VMEM)
    shape = jax.ShapeDtypeStruct((2 * tokens + 32, HD), jnp.bfloat16)
    return pl.pallas_call(
        pack_kernel,
        grid_spec=pltpu.PrefetchScalarGridSpec(
            num_scalar_prefetch=1, grid=(), in_specs=[vmem] * 4, out_specs=[vmem] * 2
        ),
        out_shape=[shape, shape],
    )(dp.reshape(1), cotangent, gain_query.reshape(1, -1), gain_key.reshape(1, -1), mask)


def core_sum_kernel(y_ref, kept_ref, got_ref, send_ref, keep_ref):
    y = y_ref[0]
    keep_ref[...] = kept_ref[y] + got_ref[y].astype(jnp.float32)
    send_ref[...] = (kept_ref[1 - y] + got_ref[1 - y].astype(jnp.float32)).astype(send_ref.dtype)


def core_sum(y, kept, got):
    vmem = pl.BlockSpec(memory_space=pltpu.VMEM)
    return pl.pallas_call(
        core_sum_kernel,
        grid_spec=pltpu.PrefetchScalarGridSpec(
            num_scalar_prefetch=1, grid=(), in_specs=[vmem] * 2, out_specs=[vmem] * 2
        ),
        out_shape=[
            jax.ShapeDtypeStruct(kept.shape[1:], jnp.bfloat16),
            jax.ShapeDtypeStruct(kept.shape[1:], jnp.float32),
        ],
    )(y.reshape(1), kept, got)


def row_sum_kernel(z_ref, kept_ref, got_ref, keep_ref, *send_refs):
    z = z_ref[0]
    keep_ref[...] = kept_ref[z] + got_ref[z].astype(jnp.float32)
    for bit, send_ref in enumerate(send_refs, 1):
        other = z ^ bit
        send_ref[...] = (kept_ref[other] + got_ref[other].astype(jnp.float32)).astype(send_ref.dtype)


def row_sum(z, kept, got):
    vmem = pl.BlockSpec(memory_space=pltpu.VMEM)
    return pl.pallas_call(
        row_sum_kernel,
        grid_spec=pltpu.PrefetchScalarGridSpec(
            num_scalar_prefetch=1, grid=(), in_specs=[vmem] * 2, out_specs=[vmem] * 4
        ),
        out_shape=[jax.ShapeDtypeStruct(kept.shape[1:], jnp.float32)]
        + [jax.ShapeDtypeStruct(kept.shape[1:], jnp.bfloat16)] * 3,
    )(z.reshape(1), kept, got)


NN = (((1,), (0,)), ((), ()))
NT = (((1,), (1,)), ((), ()))
TN = (((0,), (0,)), ((), ()))


def dot(left, right, dims):
    return lax.dot_general(left, right, dims, preferred_element_type=jnp.float32)


def halves(values):
    high = values.astype(jnp.bfloat16)
    return high, (values - high.astype(jnp.float32)).astype(jnp.bfloat16)


def dot_fine(left, right, dims):
    return (
        dot(left[0], right[0], dims) + dot(left[0], right[1], dims) + dot(left[1], right[0], dims)
    )


def row_mean(values):
    return jnp.mean(values, axis=1, keepdims=True)


def row_total(values):
    return jnp.sum(values, axis=1, keepdims=True)


def attention_kernel(
    which_ref, kept_ref, near_ref, mid_ref, far_ref, first_ref, second_ref, out_ref, grad_ref
):
    f32, bf16 = jnp.float32, jnp.bfloat16
    tokens = kept_ref.shape[0]
    scale = HD ** (-0.5)
    message = jnp.where(which_ref[0] == 0, first_ref[...], second_ref[...])
    joined = kept_ref[...] + near_ref[...].astype(f32) + mid_ref[...].astype(f32)
    joined = (joined + far_ref[...].astype(f32)).astype(bf16)
    cot_one = message[:tokens]
    cot_two = message[tokens : 2 * tokens]
    gains = message[2 * tokens : 2 * tokens + 16].astype(f32)
    gain_query = gains[0:1] + gains[1:2] + gains[2:3]
    gain_key = gains[3:4] + gains[4:5] + gains[5:6]
    mask = message[2 * tokens + 16 :]

    rows = lax.broadcasted_iota(jnp.int32, (tokens, 16), 0) // 64
    picks = (rows == lax.broadcasted_iota(jnp.int32, (tokens, 16), 1)).astype(f32).astype(bf16)
    columns = lax.broadcasted_iota(jnp.int32, (HD, tokens), 1) // 64
    spots = (columns == lax.broadcasted_iota(jnp.int32, (HD, tokens), 0)).astype(f32).astype(bf16)
    opened = dot(dot(picks, mask, NN).astype(bf16), spots, NN) > 0.5
    query_at = lax.broadcasted_iota(jnp.int32, (tokens, tokens), 0)
    key_at = lax.broadcasted_iota(jnp.int32, (tokens, tokens), 1)
    allowed = (query_at // 64 == key_at // 64) | opened
    first = allowed & (key_at <= query_at)
    second = allowed & (key_at < query_at)

    values = joined.astype(f32)
    inverse = lax.rsqrt(row_mean(values * values) + EPS)
    normed = values * inverse
    queries = halves(normed * gain_query)
    keys = halves(normed * gain_key)
    scores = jnp.where(first, dot_fine(queries, keys, NT) * scale, -jnp.inf)
    expo = jnp.exp(scores - jnp.max(scores, axis=1, keepdims=True))
    soft_one = expo * (1.0 / row_total(expo))
    weights_one = soft_one.astype(bf16)
    step_one = dot(weights_one, joined, NN).astype(bf16)
    out_ref[0] = step_one

    step = step_one.astype(f32)
    inverse_two = lax.rsqrt(row_mean(step * step) + EPS)
    renormed = step * inverse_two
    query_two = renormed * gain_query
    own_key = renormed * gain_key
    queries_two = halves(query_two)
    scores = jnp.where(second, dot_fine(queries_two, keys, NT) * scale, -jnp.inf)
    own_score = row_total(query_two * own_key) * scale
    top = jnp.maximum(jnp.max(scores, axis=1, keepdims=True), own_score)
    expo = jnp.exp(scores - top)
    own_expo = jnp.exp(own_score - top)
    share = 1.0 / (row_total(expo) + own_expo)
    soft_two = expo * share
    own_soft = own_expo * share
    weights_two = soft_two.astype(bf16)
    step_two = dot(weights_two, joined, NN) + own_soft * step
    out_ref[1] = step_two.astype(bf16)

    d_two = cot_two.astype(f32)
    d_soft = dot(cot_two, joined, NT).astype(bf16).astype(f32)
    d_joined = dot(weights_two, cot_two, TN)
    d_own = row_total(d_two * step)
    d_step = own_soft * d_two
    shared = row_total(soft_two * d_soft) + own_soft * d_own
    d_scores = halves(soft_two * (d_soft - shared) * scale)
    d_own_score = own_soft * (d_own - shared) * scale
    d_query = dot_fine(d_scores, keys, NN) + d_own_score * own_key
    d_keys = dot_fine(d_scores, queries_two, TN)
    d_renormed = d_query * gain_query + d_own_score * query_two * gain_key
    d_step = d_step + inverse_two * (d_renormed - renormed * row_mean(d_renormed * renormed))
    d_one = (d_step.astype(bf16).astype(f32) + cot_one.astype(f32)).astype(bf16)
    d_soft = dot(d_one, joined, NT).astype(bf16).astype(f32)
    d_joined = d_joined + dot(weights_one, d_one, TN)
    d_scores = halves(soft_one * (d_soft - row_total(soft_one * d_soft)) * scale)
    d_query = dot_fine(d_scores, keys, NN)
    d_keys = d_keys + dot_fine(d_scores, queries, TN)
    d_normed = d_query * gain_query + d_keys * gain_key
    d_joined = d_joined + inverse * (d_normed - normed * row_mean(d_normed * normed))
    grad_ref[...] = d_joined.T.astype(bf16)


def attention(which, kept, pieces, messages):
    tokens = kept.shape[0]
    vmem = pl.BlockSpec(memory_space=pltpu.VMEM)
    return pl.pallas_call(
        attention_kernel,
        grid_spec=pltpu.PrefetchScalarGridSpec(
            num_scalar_prefetch=1, grid=(), in_specs=[vmem] * 6, out_specs=[vmem] * 2
        ),
        out_shape=[
            jax.ShapeDtypeStruct((2, tokens, HD), jnp.bfloat16),
            jax.ShapeDtypeStruct((HD, tokens), jnp.bfloat16),
        ],
        compiler_params=pltpu.CompilerParams(vmem_limit_bytes=24 << 20),
        cost_estimate=pl.CostEstimate(
            flops=24 * 2 * tokens * tokens * HD,
            bytes_accessed=16 * tokens * HD,
            transcendentals=2 * tokens * tokens,
        ),
    )(which.astype(jnp.int32).reshape(1), kept, *pieces, *messages)


def keep_weights_plan(hidden, fc_weight, gain_query, gain_key, block_mask, cotangent):
    me_dp = lax.axis_index("dp")
    me_z = lax.axis_index("mp")
    me_y = lax.axis_index("section") >> 1
    me_c = lax.axis_index("section") & 1
    upper = me_z >> 1
    over_x = swap("dp", 2, 1)
    over_y = swap("section", 4, 2)
    over_c = swap("section", 4, 1)
    over_z = [swap("mp", 4, bit) for bit in range(4)]

    def route(r):
        return [
            (4 * d + 2 * e + b, 4 * e + 2 * (d ^ r) + b)
            for d in range(2)
            for e in range(2)
            for b in range(2)
        ]

    hidden_other = over_x(hidden)
    messages = pack(me_dp, cotangent, gain_query, gain_key, block_mask)
    messages = [lax.ppermute(messages[r], ("dp", "mp"), route(r)) for r in range(2)]
    own_at = upper ^ me_dp

    def scatter_sum(tokens_in):
        sent = half_product(tokens_in, fc_weight, 1 - me_c, jnp.bfloat16)
        kept = half_product(tokens_in, fc_weight, me_c, jnp.float32)
        send, kept = core_sum(me_y, kept, over_c(sent))
        kept, *send = row_sum(me_z, kept, over_y(send))
        return kept, [over_z[b](send[b - 1]) for b in (1, 2, 3)]

    def spread(piece):
        part = jnp.stack([piece] + [over_z[b](piece) for b in (1, 2, 3)])
        rest = over_y(part)
        return (part, over_c(part)), (rest, over_c(rest))

    out_own, d_own = attention(own_at, *scatter_sum(hidden), messages)
    out_other, d_other = attention(1 - own_at, *scatter_sum(hidden_other), messages)
    own_parts = spread(d_own)
    other_parts = spread(d_other)

    rows = fc_weight.shape[0]
    fc_grad = None
    for flip in range(2):
        heads = []
        for core in (me_c, 1 - me_c):
            z = me_z ^ jnp.arange(4)
            heads.append(2 * (4 * (z & 1) + 2 * (me_y ^ flip) + core) + (z >> 1))
        table = jnp.concatenate(heads).astype(jnp.int32)
        fc_grad = grad_rows(
            table, own_parts[flip], other_parts[flip], hidden, hidden_other, rows, fc_grad
        )
    back = []
    for r in range(2):
        sent = jnp.where(own_at == r, out_own, out_other)
        back.append(lax.ppermute(sent, ("dp", "mp"), [(b, a) for a, b in route(r)]))
    low = jnp.where(me_dp == 0, back[0], back[1])
    high = jnp.where(me_dp == 0, back[1], back[0])
    ttt_out = jnp.concatenate([low, high], axis=2)
    return (ttt_out, fc_grad)


def per_device(sizes, hidden, fc_weight, *rest):
    heads = fc_weight.shape[0] // HD
    if sizes == (2, 4, 4) and heads == 16 and rest[0].shape[0] == 2 * HD:
        return keep_weights_plan(hidden, fc_weight, *rest)
    return gather_weights_plan(hidden, fc_weight, *rest)


def solution(mesh):
    in_specs = (
        P("dp", ("mp", "section")),
        P("dp", ("mp", "section")),
        P(("mp", "section")),
        P(("mp", "section")),
        P("dp", None),
        P(None, "dp", ("mp", "section")),
    )
    out_specs = (P(None, "dp", ("mp", "section")), P("dp", ("mp", "section")))
    sizes = tuple(mesh.shape[name] for name in ("dp", "mp", "section"))
    return jax.shard_map(
        partial(per_device, sizes), mesh=mesh, in_specs=in_specs, out_specs=out_specs, check_vma=False
    )
```

```python
from functools import partial

import jax
import jax.numpy as jnp
from jax import lax
from jax.experimental import pallas as pl
from jax.experimental.pallas import tpu as pltpu
from jax.sharding import PartitionSpec as P

HD = 128


EPS = 1e-06


def rms_scale(values):
    return values * lax.rsqrt(jnp.mean(values * values, axis=-1, keepdims=True) + EPS)


def visible_sets(block_mask, length):
    position = jnp.arange(length, dtype=jnp.int32)
    block_of = position // 64
    onehot = (
        block_of[:, None] == jnp.arange(block_mask.shape[0], dtype=jnp.int32)[None, :]
    ).astype(jnp.float32)
    opened = (
        jnp.dot(
            jnp.dot(onehot, block_mask.astype(jnp.float32), precision=lax.Precision.HIGHEST),
            onehot.T,
            precision=lax.Precision.HIGHEST,
        )
        > 0.5
    )
    earlier = block_of[None, :] < block_of[:, None]
    same_block = block_of[None, :] == block_of[:, None]
    causal = position[None, :] <= position[:, None]
    first = causal & (same_block | opened & earlier)
    second = first & (position[None, :] < position[:, None])
    return (first, second)


def head_steps(joined_head, gain_query, gain_key, first, second):
    scale = joined_head.shape[-1] ** (-0.5)
    normed = rms_scale(joined_head.astype(jnp.float32))
    queries = normed * gain_query
    keys_ctx = normed * gain_key
    scores = jnp.dot(queries, keys_ctx.T, precision=lax.Precision.HIGHEST) * scale
    scores = jnp.where(first, scores, -jnp.inf)
    top_one = jnp.max(scores, axis=-1, keepdims=True)
    expo_one = jnp.exp(scores - top_one)
    weights_one = (expo_one / jnp.sum(expo_one, axis=-1, keepdims=True)).astype(jnp.bfloat16)
    step_one = jnp.dot(weights_one, joined_head, preferred_element_type=jnp.float32).astype(
        jnp.bfloat16
    )
    renorm = rms_scale(step_one.astype(jnp.float32))
    queries_two = renorm * gain_query
    own_key = renorm * gain_key
    scores_two = jnp.dot(queries_two, keys_ctx.T, precision=lax.Precision.HIGHEST) * scale
    scores_two = jnp.where(second, scores_two, -jnp.inf)
    own_score = jnp.sum(queries_two * own_key, axis=-1) * scale
    top_two = jnp.maximum(jnp.max(scores_two, axis=-1), own_score)
    expo_two = jnp.exp(scores_two - top_two[:, None])
    own_expo = jnp.exp(own_score - top_two)
    total = jnp.sum(expo_two, axis=-1) + own_expo
    weights_two = (expo_two / total[:, None]).astype(jnp.bfloat16)
    step_two = jnp.dot(weights_two, joined_head, preferred_element_type=jnp.float32) + (
        own_expo / total
    )[:, None] * step_one.astype(jnp.float32)
    return (step_one, step_two.astype(jnp.bfloat16))


def sequence_steps(joined_seq, gain_query, gain_key, block_mask):
    length, width = joined_seq.shape
    heads = width // HD
    first, second = visible_sets(block_mask, length)
    split = joined_seq.reshape(length, heads, HD).transpose(1, 0, 2)
    one_out, two_out = jax.vmap(head_steps, in_axes=(0, 0, 0, None, None))(
        split, gain_query.reshape(heads, HD), gain_key.reshape(heads, HD), first, second
    )
    return (
        one_out.transpose(1, 0, 2).reshape(length, width),
        two_out.transpose(1, 0, 2).reshape(length, width),
    )


def sequence_train(joined_seq, gain_query, gain_key, block_mask, cot_one, cot_two):
    forward = partial(
        sequence_steps, gain_query=gain_query, gain_key=gain_key, block_mask=block_mask
    )
    outputs, pullback = jax.vjp(forward, joined_seq)
    grads = pullback((cot_one, cot_two))
    return (outputs[0], outputs[1], grads[0])


def gather_weights_plan(hidden, fc_weight, gain_query, gain_key, block_mask, cotangent):
    partial_joined = lax.dot_general(
        hidden,
        lax.all_gather(fc_weight, "dp", axis=0, tiled=True),
        (((1,), (1,)), ((), ())),
        preferred_element_type=jnp.float32,
    )
    joined = lax.psum_scatter(
        partial_joined, ("mp", "section"), scatter_dimension=1, tiled=True
    ).astype(jnp.bfloat16)
    step_one, step_two, d_joined = sequence_train(
        joined, gain_query, gain_key, block_mask, cotangent[0], cotangent[1]
    )
    ttt_out = jnp.stack([step_one, step_two])
    grad_full = lax.all_gather(d_joined, ("mp", "section"), axis=1, tiled=True)
    fc_grad = lax.psum_scatter(
        lax.dot_general(
            grad_full, hidden, (((0,), (0,)), ((), ())), preferred_element_type=jnp.float32
        ),
        "dp",
        scatter_dimension=0,
        tiled=True,
    )
    return (ttt_out, fc_grad)


def after(array, *others):
    return lax.optimization_barrier((array, *others))[0]


def swap(axis, size, bit):
    return lambda array: lax.ppermute(array, axis, [(i, i ^ bit) for i in range(size)])


def tile_product(hidden, weight_rows, out_ref, y, z0):
    product = lax.dot_general(
        hidden, weight_rows, (((1,), (1,)), ((), ())), preferred_element_type=jnp.float32
    )
    out_ref[y, z0] = product[:, :HD].astype(out_ref.dtype)
    out_ref[y, 2 + z0] = product[:, HD:].astype(out_ref.dtype)


def streamed_product_kernel(core_ref, hidden_ref, weight_ref, out_ref, held, rows, sems):
    loads = [pltpu.make_async_copy(hidden_ref, held, sems.at[4])]
    for y in range(2):
        for z0 in range(2):
            row = pl.multiple_of((4 * z0 + 2 * y + core_ref[0]) * 2 * HD, 2 * HD)
            slot = 2 * y + z0
            loads.append(
                pltpu.make_async_copy(
                    weight_ref.at[pl.ds(row, 2 * HD)], rows.at[slot], sems.at[slot]
                )
            )
    for load in loads:
        load.start()
    for load in loads:
        load.wait()
    for y in range(2):
        for z0 in range(2):
            tile_product(held[...], rows[2 * y + z0], out_ref, y, z0)


def streamed_product(hidden, weight, core, dtype):
    tokens, features = hidden.shape
    vmem = pl.BlockSpec(memory_space=pltpu.VMEM)
    hbm = pl.BlockSpec(memory_space=pltpu.HBM)
    return pl.pallas_call(
        streamed_product_kernel,
        name="streamed_product",
        grid_spec=pltpu.PrefetchScalarGridSpec(
            num_scalar_prefetch=1,
            grid=(),
            in_specs=[hbm, hbm],
            out_specs=vmem,
            scratch_shapes=[
                pltpu.VMEM((tokens, features), hidden.dtype),
                pltpu.VMEM((4, 2 * HD, features), weight.dtype),
                pltpu.SemaphoreType.DMA((5,)),
            ],
        ),
        out_shape=jax.ShapeDtypeStruct((2, 4, tokens, HD), dtype),
        compiler_params=pltpu.CompilerParams(vmem_limit_bytes=12 << 20),
        cost_estimate=pl.CostEstimate(
            flops=2 * tokens * features * 8 * HD,
            bytes_accessed=2 * features * 8 * HD + 2 * tokens * features,
            transcendentals=0,
        ),
    )(
        core.reshape(1),
        pltpu.with_memory_space_constraint(hidden, pltpu.HBM),
        pltpu.with_memory_space_constraint(weight, pltpu.HBM),
    )


def load_kernel(core_ref, weight_ref, send_ref, keep_ref, sems):
    copies = []
    for half, store_ref in enumerate((send_ref, keep_ref)):
        core = (1 - core_ref[0]) if half == 0 else core_ref[0]
        for y in range(2):
            for z0 in range(2):
                row = pl.multiple_of((4 * z0 + 2 * y + core) * 2 * HD, 2 * HD)
                slot = 2 * y + z0
                copy = pltpu.make_async_copy(
                    weight_ref.at[pl.ds(row, 2 * HD)], store_ref.at[slot], sems.at[4 * half + slot]
                )
                copy.start()
                copies.append(copy)
    for copy in copies:
        copy.wait()


def load_weights(weight, core):
    vmem = pl.BlockSpec(memory_space=pltpu.VMEM)
    half = jax.ShapeDtypeStruct((4, 2 * HD, weight.shape[1]), weight.dtype)
    return pl.pallas_call(
        load_kernel,
        name="load_weights",
        grid_spec=pltpu.PrefetchScalarGridSpec(
            num_scalar_prefetch=1,
            grid=(),
            in_specs=[pl.BlockSpec(memory_space=pltpu.HBM)],
            out_specs=[vmem] * 2,
            scratch_shapes=[pltpu.SemaphoreType.DMA((8,))],
        ),
        out_shape=[half, half],
        compiler_params=pltpu.CompilerParams(vmem_limit_bytes=14 << 20),
    )(core.reshape(1), pltpu.with_memory_space_constraint(weight, pltpu.HBM))


def half_product_kernel(hidden_ref, store_ref, out_ref):
    for y in range(2):
        for z0 in range(2):
            tile_product(hidden_ref[...], store_ref[2 * y + z0], out_ref, y, z0)


def half_product(hidden, store, dtype):
    tokens, features = hidden.shape
    vmem = pl.BlockSpec(memory_space=pltpu.VMEM)
    return pl.pallas_call(
        half_product_kernel,
        in_specs=[vmem] * 2,
        out_specs=vmem,
        out_shape=jax.ShapeDtypeStruct((2, 4, tokens, HD), dtype),
        compiler_params=pltpu.CompilerParams(vmem_limit_bytes=8 << 20),
        cost_estimate=pl.CostEstimate(
            flops=2 * tokens * features * 8 * HD,
            bytes_accessed=2 * features * 8 * HD + 2 * tokens * features,
            transcendentals=0,
        ),
        name="half_product",
    )(hidden, store)


def fill_rows(table_ref, pieces, hidden_ref, hidden_other_ref, out_ref, total, sems):
    copies = []
    for g in range(4):
        left = jnp.concatenate([pieces[g // 2][2 * (g % 2) + i] for i in range(2)], axis=0)
        right = jnp.concatenate([pieces[2 + g // 2][2 * (g % 2) + i] for i in range(2)], axis=0)
        total[g] = jnp.dot(left, hidden_ref[...], preferred_element_type=jnp.float32) + jnp.dot(
            right, hidden_other_ref[...], preferred_element_type=jnp.float32
        )
        for i in range(2):
            row = pl.multiple_of(table_ref[2 * g + i] * HD, HD)
            copy = pltpu.make_async_copy(
                total.at[g, pl.ds(i * HD, HD)], out_ref.at[pl.ds(row, HD)], sems.at[2 * g + i]
            )
            copy.start()
            copies.append(copy)
    return copies


def grad_kernel(table_ref, *refs):
    pieces, hiddens, (out_ref, token_ref), scratch = refs[:4], refs[4:6], refs[6:8], refs[8:]
    copies = fill_rows(table_ref, pieces, *hiddens, out_ref, *scratch)
    token_ref[...] = jnp.zeros_like(token_ref)
    for copy in copies:
        copy.wait()


def last_grad_kernel(table_ref, home_ref, dp_ref, *refs):
    pieces, hiddens, outs = refs[:4], refs[4:6], refs[6:9]
    out_ref, steps_ref, *scratch = refs[11:]
    copies = fill_rows(table_ref, pieces, *hiddens, out_ref, *scratch)
    own, across, beside = (ref[...] for ref in outs)
    home = home_ref[0] == 1
    near = jnp.where(home, own, beside)
    other = jnp.where(home, beside, across)
    low = dp_ref[0] == 0
    steps_ref[:, :, :HD] = jnp.where(low, near, other)
    steps_ref[:, :, HD:] = jnp.where(low, other, near)
    for copy in copies:
        copy.wait()


def grad_rows(table, own, other, hidden, hidden_other, rows, last=None):
    tokens, features = hidden.shape
    vmem = pl.BlockSpec(memory_space=pltpu.VMEM)
    hbm = pl.BlockSpec(memory_space=pltpu.HBM)
    grads = jax.ShapeDtypeStruct((rows, features), jnp.float32)
    args = [*own, *other, hidden, hidden_other]
    if last is None:
        kernel, scalars, in_specs = grad_kernel, [table], [vmem] * 6
        out_shape, aliases = [grads, jax.ShapeDtypeStruct((8, HD), jnp.float32)], {}
    else:
        home, dp, outs, token, previous = last
        kernel, scalars = last_grad_kernel, [table, home.reshape(1), dp.reshape(1)]
        in_specs = [vmem] * 10 + [hbm]
        out_shape = [grads, jax.ShapeDtypeStruct((2, tokens, 2 * HD), jnp.bfloat16)]
        aliases = {13: 0}
        args = args + [*outs, token, previous]
    return pl.pallas_call(
        kernel,
        name="grad_rows",
        grid_spec=pltpu.PrefetchScalarGridSpec(
            num_scalar_prefetch=len(scalars),
            grid=(),
            in_specs=in_specs,
            out_specs=[hbm, vmem],
            scratch_shapes=[
                pltpu.VMEM((4, 2 * HD, features), jnp.float32),
                pltpu.SemaphoreType.DMA((8,)),
            ],
        ),
        out_shape=out_shape,
        input_output_aliases=aliases,
        compiler_params=pltpu.CompilerParams(vmem_limit_bytes=14 << 20),
        cost_estimate=pl.CostEstimate(
            flops=32 * HD * tokens * features,
            bytes_accessed=32 * HD * features,
            transcendentals=0,
        ),
    )(*scalars, *args)


def pack_kernel(head_ref, cot_ref, query_ref, key_ref, mask_ref, first_ref, second_ref):
    tokens = cot_ref.shape[1]
    for r, out_ref in enumerate((first_ref, second_ref)):
        lanes = pl.ds(pl.multiple_of((head_ref[0] ^ r) * HD, HD), HD)
        out_ref[:tokens] = cot_ref[0, :, lanes]
        out_ref[tokens : 2 * tokens] = cot_ref[1, :, lanes]
        terms = []
        for gain_ref in (query_ref, key_ref):
            rest = gain_ref[:, lanes]
            for _ in range(3):
                term = rest.astype(jnp.bfloat16).astype(jnp.float32)
                terms.append(term)
                rest = rest - term
        terms.append(jnp.zeros((10, HD), jnp.float32))
        out_ref[2 * tokens : 2 * tokens + 16] = jnp.concatenate(terms, axis=0).astype(jnp.bfloat16)
        out_ref[2 * tokens + 16 :] = mask_ref[...].astype(jnp.bfloat16)


def pack(head, cotangent, gain_query, gain_key, block_mask):
    tokens = cotangent.shape[1]
    blocks = block_mask.shape[0]
    mask = jnp.pad(block_mask.astype(jnp.float32), ((0, 16 - blocks), (0, HD - blocks)))
    vmem = pl.BlockSpec(memory_space=pltpu.VMEM)
    shape = jax.ShapeDtypeStruct((2 * tokens + 32, HD), jnp.bfloat16)
    return pl.pallas_call(
        pack_kernel,
        name="pack",
        grid_spec=pltpu.PrefetchScalarGridSpec(
            num_scalar_prefetch=1, grid=(), in_specs=[vmem] * 4, out_specs=[vmem] * 2
        ),
        out_shape=[shape, shape],
        compiler_params=pltpu.CompilerParams(vmem_limit_bytes=4 << 20),
    )(head.reshape(1), cotangent, gain_query.reshape(1, -1), gain_key.reshape(1, -1), mask)


def core_sum_kernel(y_ref, kept_ref, got_ref, send_ref, keep_ref):
    y = y_ref[0]
    keep_ref[...] = kept_ref[y] + got_ref[y].astype(jnp.float32)
    send_ref[...] = (kept_ref[1 - y] + got_ref[1 - y].astype(jnp.float32)).astype(send_ref.dtype)


def core_sum(y, kept, got):
    vmem = pl.BlockSpec(memory_space=pltpu.VMEM)
    return pl.pallas_call(
        core_sum_kernel,
        name="core_sum",
        grid_spec=pltpu.PrefetchScalarGridSpec(
            num_scalar_prefetch=1, grid=(), in_specs=[vmem] * 2, out_specs=[vmem] * 2
        ),
        out_shape=[
            jax.ShapeDtypeStruct(kept.shape[1:], jnp.bfloat16),
            jax.ShapeDtypeStruct(kept.shape[1:], jnp.float32),
        ],
        compiler_params=pltpu.CompilerParams(vmem_limit_bytes=4 << 20),
    )(y.reshape(1), kept, got)


def row_sum_kernel(z_ref, kept_ref, got_ref, keep_ref, *send_refs):
    z = z_ref[0]
    keep_ref[...] = kept_ref[z] + got_ref[z].astype(jnp.float32)
    for bit, send_ref in enumerate(send_refs, 1):
        other = z ^ bit
        send_ref[...] = (kept_ref[other] + got_ref[other].astype(jnp.float32)).astype(send_ref.dtype)


def row_sum(z, kept, got):
    vmem = pl.BlockSpec(memory_space=pltpu.VMEM)
    return pl.pallas_call(
        row_sum_kernel,
        name="row_sum",
        grid_spec=pltpu.PrefetchScalarGridSpec(
            num_scalar_prefetch=1, grid=(), in_specs=[vmem] * 2, out_specs=[vmem] * 4
        ),
        out_shape=[jax.ShapeDtypeStruct(kept.shape[1:], jnp.float32)]
        + [jax.ShapeDtypeStruct(kept.shape[1:], jnp.bfloat16)] * 3,
        compiler_params=pltpu.CompilerParams(vmem_limit_bytes=4 << 20),
    )(z.reshape(1), kept, got)


NN = (((1,), (0,)), ((), ()))
NT = (((1,), (1,)), ((), ()))
TN = (((0,), (0,)), ((), ()))


def dot(left, right, dims):
    return lax.dot_general(left, right, dims, preferred_element_type=jnp.float32)


def halves(values):
    high = values.astype(jnp.bfloat16)
    return high, (values - high.astype(jnp.float32)).astype(jnp.bfloat16)


def dot_fine(left, right, dims):
    return (
        dot(left[0], right[0], dims) + dot(left[0], right[1], dims) + dot(left[1], right[0], dims)
    )


def row_mean(values):
    return jnp.mean(values, axis=1, keepdims=True)


def row_total(values):
    return jnp.sum(values, axis=1, keepdims=True)


def attention_kernel(
    which_ref, kept_ref, near_ref, mid_ref, far_ref, first_ref, second_ref, out_ref, grad_ref
):
    f32, bf16 = jnp.float32, jnp.bfloat16
    tokens = kept_ref.shape[0]
    scale = HD ** (-0.5)
    message = jnp.where(which_ref[0] == 1, first_ref[...], second_ref[...])
    joined = kept_ref[...] + near_ref[...].astype(f32) + mid_ref[...].astype(f32)
    joined = (joined + far_ref[...].astype(f32)).astype(bf16)
    cot_one = message[:tokens]
    cot_two = message[tokens : 2 * tokens]
    gains = message[2 * tokens : 2 * tokens + 16].astype(f32)
    gain_query = gains[0:1] + gains[1:2] + gains[2:3]
    gain_key = gains[3:4] + gains[4:5] + gains[5:6]
    mask = message[2 * tokens + 16 :]

    rows = lax.broadcasted_iota(jnp.int32, (tokens, 16), 0) // 64
    picks = (rows == lax.broadcasted_iota(jnp.int32, (tokens, 16), 1)).astype(f32).astype(bf16)
    columns = lax.broadcasted_iota(jnp.int32, (HD, tokens), 1) // 64
    spots = (columns == lax.broadcasted_iota(jnp.int32, (HD, tokens), 0)).astype(f32).astype(bf16)
    opened = dot(dot(picks, mask, NN).astype(bf16), spots, NN) > 0.5
    query_at = lax.broadcasted_iota(jnp.int32, (tokens, tokens), 0)
    key_at = lax.broadcasted_iota(jnp.int32, (tokens, tokens), 1)
    allowed = (query_at // 64 == key_at // 64) | opened
    first = allowed & (key_at <= query_at)
    second = allowed & (key_at < query_at)

    values = joined.astype(f32)
    inverse = lax.rsqrt(row_mean(values * values) + EPS)
    normed = values * inverse
    queries = halves(normed * gain_query)
    keys = halves(normed * gain_key)
    scores = jnp.where(first, dot_fine(queries, keys, NT) * scale, -jnp.inf)
    expo = jnp.exp(scores - jnp.max(scores, axis=1, keepdims=True))
    soft_one = expo * (1.0 / row_total(expo))
    weights_one = soft_one.astype(bf16)
    step_one = dot(weights_one, joined, NN).astype(bf16)

    step_values = step_one.astype(f32)
    inverse_two = lax.rsqrt(row_mean(step_values * step_values) + EPS)
    renormed = step_values * inverse_two
    query_two = renormed * gain_query
    own_key = renormed * gain_key
    queries_two = halves(query_two)
    scores = jnp.where(second, dot_fine(queries_two, keys, NT) * scale, -jnp.inf)
    own_score = row_total(query_two * own_key) * scale
    top = jnp.maximum(jnp.max(scores, axis=1, keepdims=True), own_score)
    expo = jnp.exp(scores - top)
    own_expo = jnp.exp(own_score - top)
    share = 1.0 / (row_total(expo) + own_expo)
    soft_two = expo * share
    own_soft = own_expo * share
    weights_two = soft_two.astype(bf16)
    step_two = dot(weights_two, joined, NN) + own_soft * step_values
    out_ref[0] = step_one
    out_ref[1] = step_two.astype(bf16)

    d_two = cot_two.astype(f32)
    d_soft = dot(cot_two, joined, NT).astype(bf16).astype(f32)
    d_joined = dot(weights_two, cot_two, TN)
    d_own = row_total(d_two * step_values)
    d_step = own_soft * d_two
    shared = row_total(soft_two * d_soft) + own_soft * d_own
    d_scores = halves(soft_two * (d_soft - shared) * scale)
    d_own_score = own_soft * (d_own - shared) * scale
    d_query = dot_fine(d_scores, keys, NN) + d_own_score * own_key
    d_keys = dot_fine(d_scores, queries_two, TN)
    d_renormed = d_query * gain_query + d_own_score * query_two * gain_key
    d_step = d_step + inverse_two * (d_renormed - renormed * row_mean(d_renormed * renormed))
    d_one = (d_step.astype(bf16).astype(f32) + cot_one.astype(f32)).astype(bf16)
    d_soft = dot(d_one, joined, NT).astype(bf16).astype(f32)
    d_joined = d_joined + dot(weights_one, d_one, TN)
    d_scores = halves(soft_one * (d_soft - row_total(soft_one * d_soft)) * scale)
    d_query = dot_fine(d_scores, keys, NN)
    d_keys = d_keys + dot_fine(d_scores, queries, TN)
    d_normed = d_query * gain_query + d_keys * gain_key
    d_joined = d_joined + inverse * (d_normed - normed * row_mean(d_normed * normed))
    grad_ref[...] = d_joined.T.astype(bf16)


def attention(home, kept, pieces, messages):
    tokens = kept.shape[0]
    vmem = pl.BlockSpec(memory_space=pltpu.VMEM)
    return pl.pallas_call(
        attention_kernel,
        name="attention",
        grid_spec=pltpu.PrefetchScalarGridSpec(
            num_scalar_prefetch=1, grid=(), in_specs=[vmem] * 6, out_specs=[vmem] * 2
        ),
        out_shape=[
            jax.ShapeDtypeStruct((2, tokens, HD), jnp.bfloat16),
            jax.ShapeDtypeStruct((HD, tokens), jnp.bfloat16),
        ],
        compiler_params=pltpu.CompilerParams(vmem_limit_bytes=12 << 20),
        cost_estimate=pl.CostEstimate(
            flops=24 * 2 * tokens * tokens * HD,
            bytes_accessed=16 * tokens * HD,
            transcendentals=2 * tokens * tokens,
        ),
    )(home.reshape(1), kept, *pieces, *messages)


def keep_weights_plan(hidden, fc_weight, gain_query, gain_key, block_mask, cotangent):
    me_dp = lax.axis_index("dp")
    me_z = lax.axis_index("mp")
    me_y = lax.axis_index("section") >> 1
    me_c = lax.axis_index("section") & 1
    over_x = swap("dp", 2, 1)
    over_y = swap("section", 4, 2)
    over_c = swap("section", 4, 1)
    over_z = [swap("mp", 4, bit) for bit in range(4)]
    at_home = (me_z >> 1) == me_dp
    home = at_home.astype(jnp.int32)

    def far_half(kept, got):
        kept, *sent = row_sum(me_z, kept, got)
        return kept, [over_z[b](sent[b - 1]) for b in (3, 2, 1)], sent

    def spread_z(piece, *first):
        return jnp.stack([piece] + [after(over_z[b](piece), *first) for b in (1, 2, 3)])

    hidden_other = over_x(hidden)
    sent = streamed_product(hidden, fc_weight, 1 - me_c, jnp.bfloat16)
    kept = streamed_product(hidden, fc_weight, me_c, jnp.float32)
    sent, kept = core_sum(me_y, kept, over_c(sent))
    got = over_y(sent)
    stay, go = pack(
        me_dp ^ (1 - home), after(cotangent, sent), gain_query, gain_key, block_mask
    )
    come = over_z[2](go)
    own_kept, own_pieces, sent = far_half(kept, got)
    stores = load_weights(after(fc_weight, go), me_c)
    crossing = jnp.where(at_home, come, stay)
    late = after(hidden_other, come, *own_pieces, *stores)
    sent = half_product(late, stores[0], jnp.bfloat16)
    kept = half_product(late, stores[1], jnp.float32)
    sent, kept = core_sum(me_y, kept, over_c(sent))
    got = over_y(sent)
    crossed = over_x(after(crossing, sent))
    out_own, d_own = attention(home, after(own_kept, sent), own_pieces, (stay, come))
    kept, pieces, sent = far_half(kept, after(got, d_own))
    own_part = spread_z(d_own, *sent)
    kept = after(kept, own_part)
    own_rest = over_y(own_part)
    out_other, d_other = attention(home, kept, pieces, (crossed, crossed))
    across = over_x(out_other)
    other_part = spread_z(d_other, across, own_rest)
    other_rest = over_y(other_part)
    beside = over_z[2](jnp.where(at_home, across, out_own))

    def table(flip):
        z = me_z ^ jnp.arange(4)
        heads = [
            2 * (4 * (z & 1) + 2 * (me_y ^ flip) + core) + (z >> 1) for core in (me_c, 1 - me_c)
        ]
        return jnp.concatenate(heads).astype(jnp.int32)

    rows = fc_weight.shape[0]
    fc_grad, token = grad_rows(
        table(0),
        (own_part, over_c(own_part)),
        (other_part, over_c(other_part)),
        hidden,
        hidden_other,
        rows,
    )
    other_rest, token, beside = lax.optimization_barrier((other_rest, token, beside))
    fc_grad, ttt_out = grad_rows(
        table(1),
        (own_rest, over_c(own_rest)),
        (other_rest, over_c(other_rest)),
        hidden,
        hidden_other,
        rows,
        (home, me_dp, (out_own, across, beside), token, fc_grad),
    )
    return (ttt_out, fc_grad)


def per_device(sizes, hidden, fc_weight, *rest):
    heads = fc_weight.shape[0] // HD
    if sizes == (2, 4, 4) and heads == 16 and rest[0].shape[0] == 2 * HD:
        return keep_weights_plan(hidden, fc_weight, *rest)
    return gather_weights_plan(hidden, fc_weight, *rest)


def solution(mesh):
    in_specs = (
        P("dp", ("mp", "section")),
        P("dp", ("mp", "section")),
        P(("mp", "section")),
        P(("mp", "section")),
        P("dp", None),
        P(None, "dp", ("mp", "section")),
    )
    out_specs = (P(None, "dp", ("mp", "section")), P("dp", ("mp", "section")))
    sizes = tuple(mesh.shape[name] for name in ("dp", "mp", "section"))
    return jax.shard_map(
        partial(per_device, sizes), mesh=mesh, in_specs=in_specs, out_specs=out_specs, check_vma=False
    )
```

```python
from functools import partial

import jax
import jax.numpy as jnp
from jax import lax
from jax.experimental import pallas as pl
from jax.experimental.pallas import tpu as pltpu
from jax.sharding import PartitionSpec as P

HD = 128


EPS = 1e-06


def rms_scale(values):
    return values * lax.rsqrt(jnp.mean(values * values, axis=-1, keepdims=True) + EPS)


def visible_sets(block_mask, length):
    position = jnp.arange(length, dtype=jnp.int32)
    block_of = position // 64
    onehot = (
        block_of[:, None] == jnp.arange(block_mask.shape[0], dtype=jnp.int32)[None, :]
    ).astype(jnp.float32)
    opened = (
        jnp.dot(
            jnp.dot(onehot, block_mask.astype(jnp.float32), precision=lax.Precision.HIGHEST),
            onehot.T,
            precision=lax.Precision.HIGHEST,
        )
        > 0.5
    )
    earlier = block_of[None, :] < block_of[:, None]
    same_block = block_of[None, :] == block_of[:, None]
    causal = position[None, :] <= position[:, None]
    first = causal & (same_block | opened & earlier)
    second = first & (position[None, :] < position[:, None])
    return (first, second)


def head_steps(joined_head, gain_query, gain_key, first, second):
    scale = joined_head.shape[-1] ** (-0.5)
    normed = rms_scale(joined_head.astype(jnp.float32))
    queries = normed * gain_query
    keys_ctx = normed * gain_key
    scores = jnp.dot(queries, keys_ctx.T, precision=lax.Precision.HIGHEST) * scale
    scores = jnp.where(first, scores, -jnp.inf)
    top_one = jnp.max(scores, axis=-1, keepdims=True)
    expo_one = jnp.exp(scores - top_one)
    weights_one = (expo_one / jnp.sum(expo_one, axis=-1, keepdims=True)).astype(jnp.bfloat16)
    step_one = jnp.dot(weights_one, joined_head, preferred_element_type=jnp.float32).astype(
        jnp.bfloat16
    )
    renorm = rms_scale(step_one.astype(jnp.float32))
    queries_two = renorm * gain_query
    own_key = renorm * gain_key
    scores_two = jnp.dot(queries_two, keys_ctx.T, precision=lax.Precision.HIGHEST) * scale
    scores_two = jnp.where(second, scores_two, -jnp.inf)
    own_score = jnp.sum(queries_two * own_key, axis=-1) * scale
    top_two = jnp.maximum(jnp.max(scores_two, axis=-1), own_score)
    expo_two = jnp.exp(scores_two - top_two[:, None])
    own_expo = jnp.exp(own_score - top_two)
    total = jnp.sum(expo_two, axis=-1) + own_expo
    weights_two = (expo_two / total[:, None]).astype(jnp.bfloat16)
    step_two = jnp.dot(weights_two, joined_head, preferred_element_type=jnp.float32) + (
        own_expo / total
    )[:, None] * step_one.astype(jnp.float32)
    return (step_one, step_two.astype(jnp.bfloat16))


def sequence_steps(joined_seq, gain_query, gain_key, block_mask):
    length, width = joined_seq.shape
    heads = width // HD
    first, second = visible_sets(block_mask, length)
    split = joined_seq.reshape(length, heads, HD).transpose(1, 0, 2)
    one_out, two_out = jax.vmap(head_steps, in_axes=(0, 0, 0, None, None))(
        split, gain_query.reshape(heads, HD), gain_key.reshape(heads, HD), first, second
    )
    return (
        one_out.transpose(1, 0, 2).reshape(length, width),
        two_out.transpose(1, 0, 2).reshape(length, width),
    )


def sequence_train(joined_seq, gain_query, gain_key, block_mask, cot_one, cot_two):
    forward = partial(
        sequence_steps, gain_query=gain_query, gain_key=gain_key, block_mask=block_mask
    )
    outputs, pullback = jax.vjp(forward, joined_seq)
    grads = pullback((cot_one, cot_two))
    return (outputs[0], outputs[1], grads[0])


def gather_weights_plan(hidden, fc_weight, gain_query, gain_key, block_mask, cotangent):
    partial_joined = lax.dot_general(
        hidden,
        lax.all_gather(fc_weight, "dp", axis=0, tiled=True),
        (((1,), (1,)), ((), ())),
        preferred_element_type=jnp.float32,
    )
    joined = lax.psum_scatter(
        partial_joined, ("mp", "section"), scatter_dimension=1, tiled=True
    ).astype(jnp.bfloat16)
    step_one, step_two, d_joined = sequence_train(
        joined, gain_query, gain_key, block_mask, cotangent[0], cotangent[1]
    )
    ttt_out = jnp.stack([step_one, step_two])
    grad_full = lax.all_gather(d_joined, ("mp", "section"), axis=1, tiled=True)
    fc_grad = lax.psum_scatter(
        lax.dot_general(
            grad_full, hidden, (((0,), (0,)), ((), ())), preferred_element_type=jnp.float32
        ),
        "dp",
        scatter_dimension=0,
        tiled=True,
    )
    return (ttt_out, fc_grad)


def after(array, *others):
    return lax.optimization_barrier((array, *others))[0]


def swap(axis, size, bit):
    return lambda array: lax.ppermute(array, axis, [(i, i ^ bit) for i in range(size)])


def tile_product(hidden, weight_rows, out_ref, y, z0):
    product = lax.dot_general(
        hidden, weight_rows, (((1,), (1,)), ((), ())), preferred_element_type=jnp.float32
    )
    out_ref[y, z0] = product[:, :HD].astype(out_ref.dtype)
    out_ref[y, 2 + z0] = product[:, HD:].astype(out_ref.dtype)


def streamed_product_kernel(core_ref, hidden_ref, weight_ref, out_ref, held, rows, sems):
    loads = [pltpu.make_async_copy(hidden_ref, held, sems.at[4])]
    for y in range(2):
        for z0 in range(2):
            row = pl.multiple_of((4 * z0 + 2 * y + core_ref[0]) * 2 * HD, 2 * HD)
            slot = 2 * y + z0
            loads.append(
                pltpu.make_async_copy(
                    weight_ref.at[pl.ds(row, 2 * HD)], rows.at[slot], sems.at[slot]
                )
            )
    for load in loads:
        load.start()
    for load in loads:
        load.wait()
    for y in range(2):
        for z0 in range(2):
            tile_product(held[...], rows[2 * y + z0], out_ref, y, z0)


def streamed_product(hidden, weight, core, dtype):
    tokens, features = hidden.shape
    vmem = pl.BlockSpec(memory_space=pltpu.VMEM)
    hbm = pl.BlockSpec(memory_space=pltpu.HBM)
    return pl.pallas_call(
        streamed_product_kernel,
        name="streamed_product",
        grid_spec=pltpu.PrefetchScalarGridSpec(
            num_scalar_prefetch=1,
            grid=(),
            in_specs=[hbm, hbm],
            out_specs=vmem,
            scratch_shapes=[
                pltpu.VMEM((tokens, features), hidden.dtype),
                pltpu.VMEM((4, 2 * HD, features), weight.dtype),
                pltpu.SemaphoreType.DMA((5,)),
            ],
        ),
        out_shape=jax.ShapeDtypeStruct((2, 4, tokens, HD), dtype),
        compiler_params=pltpu.CompilerParams(vmem_limit_bytes=12 << 20),
        cost_estimate=pl.CostEstimate(
            flops=2 * tokens * features * 8 * HD,
            bytes_accessed=2 * features * 8 * HD + 2 * tokens * features,
            transcendentals=0,
        ),
    )(
        core.reshape(1),
        pltpu.with_memory_space_constraint(hidden, pltpu.HBM),
        pltpu.with_memory_space_constraint(weight, pltpu.HBM),
    )


def load_kernel(core_ref, weight_ref, send_ref, keep_ref, sems):
    copies = []
    for half, store_ref in enumerate((send_ref, keep_ref)):
        core = (1 - core_ref[0]) if half == 0 else core_ref[0]
        for y in range(2):
            for z0 in range(2):
                row = pl.multiple_of((4 * z0 + 2 * y + core) * 2 * HD, 2 * HD)
                slot = 2 * y + z0
                copy = pltpu.make_async_copy(
                    weight_ref.at[pl.ds(row, 2 * HD)], store_ref.at[slot], sems.at[4 * half + slot]
                )
                copy.start()
                copies.append(copy)
    for copy in copies:
        copy.wait()


def load_weights(weight, core):
    vmem = pl.BlockSpec(memory_space=pltpu.VMEM)
    half = jax.ShapeDtypeStruct((4, 2 * HD, weight.shape[1]), weight.dtype)
    return pl.pallas_call(
        load_kernel,
        name="load_weights",
        grid_spec=pltpu.PrefetchScalarGridSpec(
            num_scalar_prefetch=1,
            grid=(),
            in_specs=[pl.BlockSpec(memory_space=pltpu.HBM)],
            out_specs=[vmem] * 2,
            scratch_shapes=[pltpu.SemaphoreType.DMA((8,))],
        ),
        out_shape=[half, half],
        compiler_params=pltpu.CompilerParams(vmem_limit_bytes=14 << 20),
    )(core.reshape(1), pltpu.with_memory_space_constraint(weight, pltpu.HBM))


def half_product_kernel(hidden_ref, store_ref, out_ref):
    for y in range(2):
        for z0 in range(2):
            tile_product(hidden_ref[...], store_ref[2 * y + z0], out_ref, y, z0)


def half_product(hidden, store, dtype):
    tokens, features = hidden.shape
    vmem = pl.BlockSpec(memory_space=pltpu.VMEM)
    return pl.pallas_call(
        half_product_kernel,
        in_specs=[vmem] * 2,
        out_specs=vmem,
        out_shape=jax.ShapeDtypeStruct((2, 4, tokens, HD), dtype),
        compiler_params=pltpu.CompilerParams(vmem_limit_bytes=8 << 20),
        cost_estimate=pl.CostEstimate(
            flops=2 * tokens * features * 8 * HD,
            bytes_accessed=2 * features * 8 * HD + 2 * tokens * features,
            transcendentals=0,
        ),
        name="half_product",
    )(hidden, store)


def fill_rows(table_ref, pieces, hidden_ref, hidden_other_ref, out_ref, total, sems):
    copies = []
    for head in range(8):
        side, at = divmod(head, 4)
        total[head] = jnp.dot(
            pieces[side][at], hidden_ref[...], preferred_element_type=jnp.float32
        ) + jnp.dot(pieces[2 + side][at], hidden_other_ref[...], preferred_element_type=jnp.float32)
        row = pl.multiple_of(table_ref[head] * HD, HD)
        copy = pltpu.make_async_copy(total.at[head], out_ref.at[pl.ds(row, HD)], sems.at[head])
        copy.start()
        copies.append(copy)
    return copies


def grad_kernel(table_ref, *refs):
    pieces, hiddens, (out_ref, token_ref), (total, _, sems) = refs[:4], refs[4:6], refs[6:8], refs[8:]
    copies = fill_rows(table_ref, pieces, *hiddens, out_ref, total, sems)
    token_ref[...] = jnp.zeros_like(token_ref)
    for copy in copies:
        copy.wait()


def last_grad_kernel(table_ref, home_ref, dp_ref, *refs):
    pieces, hiddens, outs = refs[:4], refs[4:6], refs[6:9]
    out_ref, steps_ref, total, steps, sems = refs[11:]
    own, across, beside = (ref[...] for ref in outs)
    home = home_ref[0] == 1
    near = jnp.where(home, own, beside)
    other = jnp.where(home, beside, across)
    low = dp_ref[0] == 0
    steps[:, :, :HD] = jnp.where(low, near, other)
    steps[:, :, HD:] = jnp.where(low, other, near)
    copies = [pltpu.make_async_copy(steps, steps_ref, sems.at[8])]
    copies[0].start()
    copies += fill_rows(table_ref, pieces, *hiddens, out_ref, total, sems)
    for copy in copies:
        copy.wait()


def grad_rows(table, own, other, hidden, hidden_other, rows, last=None):
    tokens, features = hidden.shape
    vmem = pl.BlockSpec(memory_space=pltpu.VMEM)
    hbm = pl.BlockSpec(memory_space=pltpu.HBM)
    grads = jax.ShapeDtypeStruct((rows, features), jnp.float32)
    args = [*own, *other, hidden, hidden_other]
    if last is None:
        kernel, scalars, in_specs = grad_kernel, [table], [vmem] * 6
        out_shape, aliases = [grads, jax.ShapeDtypeStruct((8, HD), jnp.float32)], {}
    else:
        home, dp, outs, token, previous = last
        kernel, scalars = last_grad_kernel, [table, home.reshape(1), dp.reshape(1)]
        in_specs = [vmem] * 10 + [hbm]
        out_shape = [grads, jax.ShapeDtypeStruct((2, tokens, 2 * HD), jnp.bfloat16)]
        aliases = {13: 0}
        args = args + [*outs, token, previous]
    return pl.pallas_call(
        kernel,
        name="grad_rows",
        grid_spec=pltpu.PrefetchScalarGridSpec(
            num_scalar_prefetch=len(scalars),
            grid=(),
            in_specs=in_specs,
            out_specs=[hbm, vmem if last is None else hbm],
            scratch_shapes=[
                pltpu.VMEM((8, HD, features), jnp.float32),
                pltpu.VMEM((2, tokens, 2 * HD), jnp.bfloat16),
                pltpu.SemaphoreType.DMA((9,)),
            ],
        ),
        out_shape=out_shape,
        input_output_aliases=aliases,
        compiler_params=pltpu.CompilerParams(vmem_limit_bytes=14 << 20),
        cost_estimate=pl.CostEstimate(
            flops=32 * HD * tokens * features,
            bytes_accessed=32 * HD * features,
            transcendentals=0,
        ),
    )(*scalars, *args)


def pack_kernel(head_ref, cot_ref, query_ref, key_ref, mask_ref, first_ref, second_ref):
    tokens = cot_ref.shape[1]
    for r, out_ref in enumerate((first_ref, second_ref)):
        lanes = pl.ds(pl.multiple_of((head_ref[0] ^ r) * HD, HD), HD)
        out_ref[:tokens] = cot_ref[0, :, lanes]
        out_ref[tokens : 2 * tokens] = cot_ref[1, :, lanes]
        terms = []
        for gain_ref in (query_ref, key_ref):
            rest = gain_ref[:, lanes]
            for _ in range(3):
                term = rest.astype(jnp.bfloat16).astype(jnp.float32)
                terms.append(term)
                rest = rest - term
        terms.append(jnp.zeros((10, HD), jnp.float32))
        out_ref[2 * tokens : 2 * tokens + 16] = jnp.concatenate(terms, axis=0).astype(jnp.bfloat16)
        out_ref[2 * tokens + 16 :] = mask_ref[...].astype(jnp.bfloat16)


def pack(head, cotangent, gain_query, gain_key, block_mask):
    tokens = cotangent.shape[1]
    blocks = block_mask.shape[0]
    mask = jnp.pad(block_mask.astype(jnp.float32), ((0, 16 - blocks), (0, HD - blocks)))
    vmem = pl.BlockSpec(memory_space=pltpu.VMEM)
    shape = jax.ShapeDtypeStruct((2 * tokens + 32, HD), jnp.bfloat16)
    return pl.pallas_call(
        pack_kernel,
        name="pack",
        grid_spec=pltpu.PrefetchScalarGridSpec(
            num_scalar_prefetch=1, grid=(), in_specs=[vmem] * 4, out_specs=[vmem] * 2
        ),
        out_shape=[shape, shape],
        compiler_params=pltpu.CompilerParams(vmem_limit_bytes=4 << 20),
    )(head.reshape(1), cotangent, gain_query.reshape(1, -1), gain_key.reshape(1, -1), mask)


def core_sum_kernel(y_ref, kept_ref, got_ref, send_ref, keep_ref):
    y = y_ref[0]
    keep_ref[...] = kept_ref[y] + got_ref[y].astype(jnp.float32)
    send_ref[...] = (kept_ref[1 - y] + got_ref[1 - y].astype(jnp.float32)).astype(send_ref.dtype)


def core_sum(y, kept, got):
    vmem = pl.BlockSpec(memory_space=pltpu.VMEM)
    return pl.pallas_call(
        core_sum_kernel,
        name="core_sum",
        grid_spec=pltpu.PrefetchScalarGridSpec(
            num_scalar_prefetch=1, grid=(), in_specs=[vmem] * 2, out_specs=[vmem] * 2
        ),
        out_shape=[
            jax.ShapeDtypeStruct(kept.shape[1:], jnp.bfloat16),
            jax.ShapeDtypeStruct(kept.shape[1:], jnp.float32),
        ],
        compiler_params=pltpu.CompilerParams(vmem_limit_bytes=4 << 20),
    )(y.reshape(1), kept, got)


def row_sum_kernel(z_ref, kept_ref, got_ref, keep_ref, *send_refs):
    z = z_ref[0]
    keep_ref[...] = kept_ref[z] + got_ref[z].astype(jnp.float32)
    for bit, send_ref in enumerate(send_refs, 1):
        other = z ^ bit
        send_ref[...] = (kept_ref[other] + got_ref[other].astype(jnp.float32)).astype(send_ref.dtype)


def row_sum(z, kept, got):
    vmem = pl.BlockSpec(memory_space=pltpu.VMEM)
    return pl.pallas_call(
        row_sum_kernel,
        name="row_sum",
        grid_spec=pltpu.PrefetchScalarGridSpec(
            num_scalar_prefetch=1, grid=(), in_specs=[vmem] * 2, out_specs=[vmem] * 4
        ),
        out_shape=[jax.ShapeDtypeStruct(kept.shape[1:], jnp.float32)]
        + [jax.ShapeDtypeStruct(kept.shape[1:], jnp.bfloat16)] * 3,
        compiler_params=pltpu.CompilerParams(vmem_limit_bytes=4 << 20),
    )(z.reshape(1), kept, got)


NN = (((1,), (0,)), ((), ()))
NT = (((1,), (1,)), ((), ()))
TN = (((0,), (0,)), ((), ()))


def dot(left, right, dims):
    return lax.dot_general(left, right, dims, preferred_element_type=jnp.float32)


def halves(values):
    high = values.astype(jnp.bfloat16)
    return high, (values - high.astype(jnp.float32)).astype(jnp.bfloat16)


def dot_fine(left, right, dims):
    return (
        dot(left[0], right[0], dims) + dot(left[0], right[1], dims) + dot(left[1], right[0], dims)
    )


def row_mean(values):
    return jnp.mean(values, axis=1, keepdims=True)


def row_total(values):
    return jnp.sum(values, axis=1, keepdims=True)


def attention_kernel(
    which_ref, kept_ref, near_ref, mid_ref, far_ref, first_ref, second_ref, out_ref, grad_ref
):
    f32, bf16 = jnp.float32, jnp.bfloat16
    tokens = kept_ref.shape[0]
    scale = HD ** (-0.5)
    message = jnp.where(which_ref[0] == 1, first_ref[...], second_ref[...])
    joined = kept_ref[...] + near_ref[...].astype(f32) + mid_ref[...].astype(f32)
    joined = (joined + far_ref[...].astype(f32)).astype(bf16)
    cot_one = message[:tokens]
    cot_two = message[tokens : 2 * tokens]
    gains = message[2 * tokens : 2 * tokens + 16].astype(f32)
    gain_query = gains[0:1] + gains[1:2] + gains[2:3]
    gain_key = gains[3:4] + gains[4:5] + gains[5:6]
    mask = message[2 * tokens + 16 :]

    rows = lax.broadcasted_iota(jnp.int32, (tokens, 16), 0) // 64
    picks = (rows == lax.broadcasted_iota(jnp.int32, (tokens, 16), 1)).astype(f32).astype(bf16)
    columns = lax.broadcasted_iota(jnp.int32, (HD, tokens), 1) // 64
    spots = (columns == lax.broadcasted_iota(jnp.int32, (HD, tokens), 0)).astype(f32).astype(bf16)
    opened = dot(dot(picks, mask, NN).astype(bf16), spots, NN) > 0.5
    query_at = lax.broadcasted_iota(jnp.int32, (tokens, tokens), 0)
    key_at = lax.broadcasted_iota(jnp.int32, (tokens, tokens), 1)
    allowed = (query_at // 64 == key_at // 64) | opened
    first = allowed & (key_at <= query_at)
    second = allowed & (key_at < query_at)

    values = joined.astype(f32)
    inverse = lax.rsqrt(row_mean(values * values) + EPS)
    normed = values * inverse
    queries = halves(normed * gain_query)
    keys = halves(normed * gain_key)
    scores = jnp.where(first, dot_fine(queries, keys, NT) * scale, -jnp.inf)
    expo = jnp.exp(scores - jnp.max(scores, axis=1, keepdims=True))
    soft_one = expo * (1.0 / row_total(expo))
    weights_one = soft_one.astype(bf16)
    step_one = dot(weights_one, joined, NN).astype(bf16)

    step_values = step_one.astype(f32)
    inverse_two = lax.rsqrt(row_mean(step_values * step_values) + EPS)
    renormed = step_values * inverse_two
    query_two = renormed * gain_query
    own_key = renormed * gain_key
    queries_two = halves(query_two)
    scores = jnp.where(second, dot_fine(queries_two, keys, NT) * scale, -jnp.inf)
    own_score = row_total(query_two * own_key) * scale
    top = jnp.maximum(jnp.max(scores, axis=1, keepdims=True), own_score)
    expo = jnp.exp(scores - top)
    own_expo = jnp.exp(own_score - top)
    share = 1.0 / (row_total(expo) + own_expo)
    soft_two = expo * share
    own_soft = own_expo * share
    weights_two = soft_two.astype(bf16)
    step_two = dot(weights_two, joined, NN) + own_soft * step_values
    out_ref[0] = step_one
    out_ref[1] = step_two.astype(bf16)

    d_two = cot_two.astype(f32)
    d_soft = dot(cot_two, joined, NT).astype(bf16).astype(f32)
    d_joined = dot(weights_two, cot_two, TN)
    d_own = row_total(d_two * step_values)
    d_step = own_soft * d_two
    shared = row_total(soft_two * d_soft) + own_soft * d_own
    d_scores = (soft_two * (d_soft - shared) * scale).astype(bf16)
    d_own_score = own_soft * (d_own - shared) * scale
    d_query = dot(d_scores, keys[0], NN) + d_own_score * own_key
    d_keys = dot(d_scores, queries_two[0], TN)
    d_renormed = d_query * gain_query + d_own_score * query_two * gain_key
    d_step = d_step + inverse_two * (d_renormed - renormed * row_mean(d_renormed * renormed))
    d_one = (d_step.astype(bf16).astype(f32) + cot_one.astype(f32)).astype(bf16)
    d_soft = dot(d_one, joined, NT).astype(bf16).astype(f32)
    d_joined = d_joined + dot(weights_one, d_one, TN)
    d_scores = (soft_one * (d_soft - row_total(soft_one * d_soft)) * scale).astype(bf16)
    d_query = dot(d_scores, keys[0], NN)
    d_keys = d_keys + dot(d_scores, queries[0], TN)
    d_normed = d_query * gain_query + d_keys * gain_key
    d_joined = d_joined + inverse * (d_normed - normed * row_mean(d_normed * normed))
    grad_ref[...] = d_joined.T.astype(bf16)


def attention(home, kept, pieces, messages):
    tokens = kept.shape[0]
    vmem = pl.BlockSpec(memory_space=pltpu.VMEM)
    return pl.pallas_call(
        attention_kernel,
        name="attention",
        grid_spec=pltpu.PrefetchScalarGridSpec(
            num_scalar_prefetch=1, grid=(), in_specs=[vmem] * 6, out_specs=[vmem] * 2
        ),
        out_shape=[
            jax.ShapeDtypeStruct((2, tokens, HD), jnp.bfloat16),
            jax.ShapeDtypeStruct((HD, tokens), jnp.bfloat16),
        ],
        compiler_params=pltpu.CompilerParams(vmem_limit_bytes=12 << 20),
        cost_estimate=pl.CostEstimate(
            flops=24 * 2 * tokens * tokens * HD,
            bytes_accessed=16 * tokens * HD,
            transcendentals=2 * tokens * tokens,
        ),
    )(home.reshape(1), kept, *pieces, *messages)


def keep_weights_plan(hidden, fc_weight, gain_query, gain_key, block_mask, cotangent):
    me_dp = lax.axis_index("dp")
    me_z = lax.axis_index("mp")
    me_y = lax.axis_index("section") >> 1
    me_c = lax.axis_index("section") & 1
    over_x = swap("dp", 2, 1)
    over_y = swap("section", 4, 2)
    over_c = swap("section", 4, 1)
    over_z = [swap("mp", 4, bit) for bit in range(4)]
    at_home = (me_z >> 1) == me_dp
    home = at_home.astype(jnp.int32)

    def far_half(kept, got, bits):
        kept, *sent = row_sum(me_z, kept, got)
        return kept, [over_z[b](sent[b - 1]) for b in bits], sent

    def spread_z(piece, *first):
        return jnp.stack([piece] + [after(over_z[b](piece), *first) for b in (1, 2, 3)])

    hidden_other = over_x(hidden)
    sent = streamed_product(hidden, fc_weight, 1 - me_c, jnp.bfloat16)
    kept = streamed_product(hidden, fc_weight, me_c, jnp.float32)
    sent, kept = core_sum(me_y, kept, over_c(sent))
    got = over_y(sent)
    stay, go = pack(
        me_dp ^ (1 - home), after(cotangent, sent), gain_query, gain_key, block_mask
    )
    come = over_z[2](go)
    stores = load_weights(after(fc_weight, go), me_c)
    own_kept, own_pieces, sent = far_half(kept, after(got, stores[0]), (3, 2, 1))
    crossing = jnp.where(at_home, come, stay)
    late = after(hidden_other, come, *stores)
    sent = half_product(late, stores[0], jnp.bfloat16)
    kept = half_product(late, stores[1], jnp.float32)
    sent = after(sent, *own_pieces)
    sent, kept = core_sum(me_y, kept, over_c(sent))
    got = over_y(sent)
    crossed = over_x(after(crossing, sent))
    out_own, d_own = attention(home, after(own_kept, sent), own_pieces, (stay, come))
    kept, pieces, sent = far_half(kept, after(got, d_own), (2, 3, 1))
    own_part = spread_z(d_own, *sent)
    kept = after(kept, own_part)
    own_rest = over_y(own_part)
    out_other, d_other = attention(home, kept, pieces, (crossed, crossed))
    across = over_x(out_other)
    other_part = spread_z(d_other, across, own_rest)
    other_rest = over_y(other_part)
    beside = over_z[2](jnp.where(at_home, across, out_own))

    def table(flip):
        z = me_z ^ jnp.arange(4)
        heads = [
            2 * (4 * (z & 1) + 2 * (me_y ^ flip) + core) + (z >> 1) for core in (me_c, 1 - me_c)
        ]
        return jnp.concatenate(heads).astype(jnp.int32)

    rows = fc_weight.shape[0]
    fc_grad, token = grad_rows(
        table(0),
        (own_part, over_c(own_part)),
        (other_part, over_c(other_part)),
        hidden,
        hidden_other,
        rows,
    )
    other_rest, token, beside = lax.optimization_barrier((other_rest, token, beside))
    fc_grad, ttt_out = grad_rows(
        table(1),
        (own_rest, over_c(own_rest)),
        (other_rest, over_c(other_rest)),
        hidden,
        hidden_other,
        rows,
        (home, me_dp, (out_own, across, beside), token, fc_grad),
    )
    return (ttt_out, fc_grad)


def per_device(sizes, hidden, fc_weight, *rest):
    heads = fc_weight.shape[0] // HD
    if sizes == (2, 4, 4) and heads == 16 and rest[0].shape[0] == 2 * HD:
        return keep_weights_plan(hidden, fc_weight, *rest)
    return gather_weights_plan(hidden, fc_weight, *rest)


def solution(mesh):
    in_specs = (
        P("dp", ("mp", "section")),
        P("dp", ("mp", "section")),
        P(("mp", "section")),
        P(("mp", "section")),
        P("dp", None),
        P(None, "dp", ("mp", "section")),
    )
    out_specs = (P(None, "dp", ("mp", "section")), P("dp", ("mp", "section")))
    sizes = tuple(mesh.shape[name] for name in ("dp", "mp", "section"))
    return jax.shard_map(
        partial(per_device, sizes), mesh=mesh, in_specs=in_specs, out_specs=out_specs, check_vma=False
    )
```

```python
from functools import partial

import jax
import jax.numpy as jnp
from jax import lax
from jax.experimental import pallas as pl
from jax.experimental.pallas import tpu as pltpu
from jax.sharding import PartitionSpec as P

HD = 128


EPS = 1e-06


def rms_scale(values):
    return values * lax.rsqrt(jnp.mean(values * values, axis=-1, keepdims=True) + EPS)


def visible_sets(block_mask, length):
    position = jnp.arange(length, dtype=jnp.int32)
    block_of = position // 64
    onehot = (
        block_of[:, None] == jnp.arange(block_mask.shape[0], dtype=jnp.int32)[None, :]
    ).astype(jnp.float32)
    opened = (
        jnp.dot(
            jnp.dot(onehot, block_mask.astype(jnp.float32), precision=lax.Precision.HIGHEST),
            onehot.T,
            precision=lax.Precision.HIGHEST,
        )
        > 0.5
    )
    earlier = block_of[None, :] < block_of[:, None]
    same_block = block_of[None, :] == block_of[:, None]
    causal = position[None, :] <= position[:, None]
    first = causal & (same_block | opened & earlier)
    second = first & (position[None, :] < position[:, None])
    return (first, second)


def head_steps(joined_head, gain_query, gain_key, first, second):
    scale = joined_head.shape[-1] ** (-0.5)
    normed = rms_scale(joined_head.astype(jnp.float32))
    queries = normed * gain_query
    keys_ctx = normed * gain_key
    scores = jnp.dot(queries, keys_ctx.T, precision=lax.Precision.HIGHEST) * scale
    scores = jnp.where(first, scores, -jnp.inf)
    top_one = jnp.max(scores, axis=-1, keepdims=True)
    expo_one = jnp.exp(scores - top_one)
    weights_one = (expo_one / jnp.sum(expo_one, axis=-1, keepdims=True)).astype(jnp.bfloat16)
    step_one = jnp.dot(weights_one, joined_head, preferred_element_type=jnp.float32).astype(
        jnp.bfloat16
    )
    renorm = rms_scale(step_one.astype(jnp.float32))
    queries_two = renorm * gain_query
    own_key = renorm * gain_key
    scores_two = jnp.dot(queries_two, keys_ctx.T, precision=lax.Precision.HIGHEST) * scale
    scores_two = jnp.where(second, scores_two, -jnp.inf)
    own_score = jnp.sum(queries_two * own_key, axis=-1) * scale
    top_two = jnp.maximum(jnp.max(scores_two, axis=-1), own_score)
    expo_two = jnp.exp(scores_two - top_two[:, None])
    own_expo = jnp.exp(own_score - top_two)
    total = jnp.sum(expo_two, axis=-1) + own_expo
    weights_two = (expo_two / total[:, None]).astype(jnp.bfloat16)
    step_two = jnp.dot(weights_two, joined_head, preferred_element_type=jnp.float32) + (
        own_expo / total
    )[:, None] * step_one.astype(jnp.float32)
    return (step_one, step_two.astype(jnp.bfloat16))


def sequence_steps(joined_seq, gain_query, gain_key, block_mask):
    length, width = joined_seq.shape
    heads = width // HD
    first, second = visible_sets(block_mask, length)
    split = joined_seq.reshape(length, heads, HD).transpose(1, 0, 2)
    one_out, two_out = jax.vmap(head_steps, in_axes=(0, 0, 0, None, None))(
        split, gain_query.reshape(heads, HD), gain_key.reshape(heads, HD), first, second
    )
    return (
        one_out.transpose(1, 0, 2).reshape(length, width),
        two_out.transpose(1, 0, 2).reshape(length, width),
    )


def sequence_train(joined_seq, gain_query, gain_key, block_mask, cot_one, cot_two):
    forward = partial(
        sequence_steps, gain_query=gain_query, gain_key=gain_key, block_mask=block_mask
    )
    outputs, pullback = jax.vjp(forward, joined_seq)
    grads = pullback((cot_one, cot_two))
    return (outputs[0], outputs[1], grads[0])


def gather_weights_plan(hidden, fc_weight, gain_query, gain_key, block_mask, cotangent):
    partial_joined = lax.dot_general(
        hidden,
        lax.all_gather(fc_weight, "dp", axis=0, tiled=True),
        (((1,), (1,)), ((), ())),
        preferred_element_type=jnp.float32,
    )
    joined = lax.psum_scatter(
        partial_joined, ("mp", "section"), scatter_dimension=1, tiled=True
    ).astype(jnp.bfloat16)
    step_one, step_two, d_joined = sequence_train(
        joined, gain_query, gain_key, block_mask, cotangent[0], cotangent[1]
    )
    ttt_out = jnp.stack([step_one, step_two])
    grad_full = lax.all_gather(d_joined, ("mp", "section"), axis=1, tiled=True)
    fc_grad = lax.psum_scatter(
        lax.dot_general(
            grad_full, hidden, (((0,), (0,)), ((), ())), preferred_element_type=jnp.float32
        ),
        "dp",
        scatter_dimension=0,
        tiled=True,
    )
    return (ttt_out, fc_grad)


def after(array, *others):
    return lax.optimization_barrier((array, *others))[0]


def swap(axis, size, bit):
    return lambda array: lax.ppermute(array, axis, [(i, i ^ bit) for i in range(size)])


def tile_product(hidden, weight_rows, out_ref, y, z0):
    product = lax.dot_general(
        hidden, weight_rows, (((1,), (1,)), ((), ())), preferred_element_type=jnp.float32
    )
    out_ref[y, z0] = product[:, :HD].astype(out_ref.dtype)
    out_ref[y, 2 + z0] = product[:, HD:].astype(out_ref.dtype)


def streamed_product_kernel(core_ref, hidden_ref, weight_ref, out_ref, held, rows, sems):
    loads = [pltpu.make_async_copy(hidden_ref, held, sems.at[4])]
    for y in range(2):
        for z0 in range(2):
            row = pl.multiple_of((4 * z0 + 2 * y + core_ref[0]) * 2 * HD, 2 * HD)
            slot = 2 * y + z0
            loads.append(
                pltpu.make_async_copy(
                    weight_ref.at[pl.ds(row, 2 * HD)], rows.at[slot], sems.at[slot]
                )
            )
    for load in loads:
        load.start()
    for load in loads:
        load.wait()
    for y in range(2):
        for z0 in range(2):
            tile_product(held[...], rows[2 * y + z0], out_ref, y, z0)


def streamed_product(hidden, weight, core, dtype):
    tokens, features = hidden.shape
    vmem = pl.BlockSpec(memory_space=pltpu.VMEM)
    hbm = pl.BlockSpec(memory_space=pltpu.HBM)
    return pl.pallas_call(
        streamed_product_kernel,
        name="streamed_product",
        grid_spec=pltpu.PrefetchScalarGridSpec(
            num_scalar_prefetch=1,
            grid=(),
            in_specs=[hbm, hbm],
            out_specs=vmem,
            scratch_shapes=[
                pltpu.VMEM((tokens, features), hidden.dtype),
                pltpu.VMEM((4, 2 * HD, features), weight.dtype),
                pltpu.SemaphoreType.DMA((5,)),
            ],
        ),
        out_shape=jax.ShapeDtypeStruct((2, 4, tokens, HD), dtype),
        compiler_params=pltpu.CompilerParams(vmem_limit_bytes=12 << 20),
        cost_estimate=pl.CostEstimate(
            flops=2 * tokens * features * 8 * HD,
            bytes_accessed=2 * features * 8 * HD + 2 * tokens * features,
            transcendentals=0,
        ),
    )(
        core.reshape(1),
        pltpu.with_memory_space_constraint(hidden, pltpu.HBM),
        pltpu.with_memory_space_constraint(weight, pltpu.HBM),
    )


def load_kernel(core_ref, weight_ref, send_ref, keep_ref, sems):
    copies = []
    for half, store_ref in enumerate((send_ref, keep_ref)):
        core = (1 - core_ref[0]) if half == 0 else core_ref[0]
        for y in range(2):
            for z0 in range(2):
                row = pl.multiple_of((4 * z0 + 2 * y + core) * 2 * HD, 2 * HD)
                slot = 2 * y + z0
                copy = pltpu.make_async_copy(
                    weight_ref.at[pl.ds(row, 2 * HD)], store_ref.at[slot], sems.at[4 * half + slot]
                )
                copy.start()
                copies.append(copy)
    for copy in copies:
        copy.wait()


def load_weights(weight, core):
    vmem = pl.BlockSpec(memory_space=pltpu.VMEM)
    half = jax.ShapeDtypeStruct((4, 2 * HD, weight.shape[1]), weight.dtype)
    return pl.pallas_call(
        load_kernel,
        name="load_weights",
        grid_spec=pltpu.PrefetchScalarGridSpec(
            num_scalar_prefetch=1,
            grid=(),
            in_specs=[pl.BlockSpec(memory_space=pltpu.HBM)],
            out_specs=[vmem] * 2,
            scratch_shapes=[pltpu.SemaphoreType.DMA((8,))],
        ),
        out_shape=[half, half],
        compiler_params=pltpu.CompilerParams(vmem_limit_bytes=14 << 20),
    )(core.reshape(1), pltpu.with_memory_space_constraint(weight, pltpu.HBM))


def half_product_kernel(hidden_ref, store_ref, out_ref):
    for y in range(2):
        for z0 in range(2):
            tile_product(hidden_ref[...], store_ref[2 * y + z0], out_ref, y, z0)


def half_product(hidden, store, dtype):
    tokens, features = hidden.shape
    vmem = pl.BlockSpec(memory_space=pltpu.VMEM)
    return pl.pallas_call(
        half_product_kernel,
        in_specs=[vmem] * 2,
        out_specs=vmem,
        out_shape=jax.ShapeDtypeStruct((2, 4, tokens, HD), dtype),
        compiler_params=pltpu.CompilerParams(vmem_limit_bytes=8 << 20),
        cost_estimate=pl.CostEstimate(
            flops=2 * tokens * features * 8 * HD,
            bytes_accessed=2 * features * 8 * HD + 2 * tokens * features,
            transcendentals=0,
        ),
        name="half_product",
    )(hidden, store)


def fill_rows(table_ref, pieces, hidden_ref, hidden_other_ref, out_ref, total, sems):
    copies = []
    for head in range(8):
        side, at = divmod(head, 4)
        total[head] = jnp.dot(
            pieces[side][at], hidden_ref[...], preferred_element_type=jnp.float32
        ) + jnp.dot(pieces[2 + side][at], hidden_other_ref[...], preferred_element_type=jnp.float32)
        row = pl.multiple_of(table_ref[head] * HD, HD)
        copy = pltpu.make_async_copy(total.at[head], out_ref.at[pl.ds(row, HD)], sems.at[head])
        copy.start()
        copies.append(copy)
    return copies


def grad_kernel(table_ref, *refs):
    pieces, hiddens, (out_ref, token_ref), (total, _, sems) = refs[:4], refs[4:6], refs[6:8], refs[8:]
    copies = fill_rows(table_ref, pieces, *hiddens, out_ref, total, sems)
    token_ref[...] = jnp.zeros_like(token_ref)
    for copy in copies:
        copy.wait()


def last_grad_kernel(table_ref, home_ref, dp_ref, *refs):
    pieces, hiddens, outs = refs[:4], refs[4:6], refs[6:9]
    out_ref, steps_ref, total, steps, sems = refs[11:]
    own, across, beside = (ref[...] for ref in outs)
    home = home_ref[0] == 1
    near = jnp.where(home, own, beside)
    other = jnp.where(home, beside, across)
    low = dp_ref[0] == 0
    steps[:, :, :HD] = jnp.where(low, near, other)
    steps[:, :, HD:] = jnp.where(low, other, near)
    copies = [pltpu.make_async_copy(steps, steps_ref, sems.at[8])]
    copies[0].start()
    copies += fill_rows(table_ref, pieces, *hiddens, out_ref, total, sems)
    for copy in copies:
        copy.wait()


def grad_rows(table, own, other, hidden, hidden_other, rows, last=None):
    tokens, features = hidden.shape
    vmem = pl.BlockSpec(memory_space=pltpu.VMEM)
    hbm = pl.BlockSpec(memory_space=pltpu.HBM)
    grads = jax.ShapeDtypeStruct((rows, features), jnp.float32)
    args = [*own, *other, hidden, hidden_other]
    if last is None:
        kernel, scalars, in_specs = grad_kernel, [table], [vmem] * 6
        out_shape, aliases = [grads, jax.ShapeDtypeStruct((8, HD), jnp.float32)], {}
    else:
        home, dp, outs, token, previous = last
        kernel, scalars = last_grad_kernel, [table, home.reshape(1), dp.reshape(1)]
        in_specs = [vmem] * 10 + [hbm]
        out_shape = [grads, jax.ShapeDtypeStruct((2, tokens, 2 * HD), jnp.bfloat16)]
        aliases = {13: 0}
        args = args + [*outs, token, previous]
    return pl.pallas_call(
        kernel,
        name="grad_rows",
        grid_spec=pltpu.PrefetchScalarGridSpec(
            num_scalar_prefetch=len(scalars),
            grid=(),
            in_specs=in_specs,
            out_specs=[hbm, vmem if last is None else hbm],
            scratch_shapes=[
                pltpu.VMEM((8, HD, features), jnp.float32),
                pltpu.VMEM((2, tokens, 2 * HD), jnp.bfloat16),
                pltpu.SemaphoreType.DMA((9,)),
            ],
        ),
        out_shape=out_shape,
        input_output_aliases=aliases,
        compiler_params=pltpu.CompilerParams(vmem_limit_bytes=14 << 20),
        cost_estimate=pl.CostEstimate(
            flops=32 * HD * tokens * features,
            bytes_accessed=32 * HD * features,
            transcendentals=0,
        ),
    )(*scalars, *args)


def pack_kernel(head_ref, cot_ref, query_ref, key_ref, mask_ref, first_ref, second_ref):
    tokens = cot_ref.shape[1]
    for r, out_ref in enumerate((first_ref, second_ref)):
        lanes = pl.ds(pl.multiple_of((head_ref[0] ^ r) * HD, HD), HD)
        out_ref[:tokens] = cot_ref[0, :, lanes]
        out_ref[tokens : 2 * tokens] = cot_ref[1, :, lanes]
        terms = []
        for gain_ref in (query_ref, key_ref):
            rest = gain_ref[:, lanes]
            for _ in range(3):
                term = rest.astype(jnp.bfloat16).astype(jnp.float32)
                terms.append(term)
                rest = rest - term
        terms.append(jnp.zeros((10, HD), jnp.float32))
        out_ref[2 * tokens : 2 * tokens + 16] = jnp.concatenate(terms, axis=0).astype(jnp.bfloat16)
        out_ref[2 * tokens + 16 :] = mask_ref[...].astype(jnp.bfloat16)


def pack(head, cotangent, gain_query, gain_key, block_mask):
    tokens = cotangent.shape[1]
    blocks = block_mask.shape[0]
    mask = jnp.pad(block_mask.astype(jnp.float32), ((0, 16 - blocks), (0, HD - blocks)))
    vmem = pl.BlockSpec(memory_space=pltpu.VMEM)
    shape = jax.ShapeDtypeStruct((2 * tokens + 32, HD), jnp.bfloat16)
    return pl.pallas_call(
        pack_kernel,
        name="pack",
        grid_spec=pltpu.PrefetchScalarGridSpec(
            num_scalar_prefetch=1, grid=(), in_specs=[vmem] * 4, out_specs=[vmem] * 2
        ),
        out_shape=[shape, shape],
        compiler_params=pltpu.CompilerParams(vmem_limit_bytes=4 << 20),
    )(head.reshape(1), cotangent, gain_query.reshape(1, -1), gain_key.reshape(1, -1), mask)


def core_sum_kernel(y_ref, kept_ref, got_ref, send_ref, keep_ref):
    y = y_ref[0]
    keep_ref[...] = kept_ref[y] + got_ref[y].astype(jnp.float32)
    send_ref[...] = (kept_ref[1 - y] + got_ref[1 - y].astype(jnp.float32)).astype(send_ref.dtype)


def core_sum(y, kept, got):
    vmem = pl.BlockSpec(memory_space=pltpu.VMEM)
    return pl.pallas_call(
        core_sum_kernel,
        name="core_sum",
        grid_spec=pltpu.PrefetchScalarGridSpec(
            num_scalar_prefetch=1, grid=(), in_specs=[vmem] * 2, out_specs=[vmem] * 2
        ),
        out_shape=[
            jax.ShapeDtypeStruct(kept.shape[1:], jnp.bfloat16),
            jax.ShapeDtypeStruct(kept.shape[1:], jnp.float32),
        ],
        compiler_params=pltpu.CompilerParams(vmem_limit_bytes=4 << 20),
    )(y.reshape(1), kept, got)


def row_sum_kernel(z_ref, kept_ref, got_ref, keep_ref, *send_refs):
    z = z_ref[0]
    keep_ref[...] = kept_ref[z] + got_ref[z].astype(jnp.float32)
    for bit, send_ref in enumerate(send_refs, 1):
        other = z ^ bit
        send_ref[...] = (kept_ref[other] + got_ref[other].astype(jnp.float32)).astype(send_ref.dtype)


def row_sum(z, kept, got):
    vmem = pl.BlockSpec(memory_space=pltpu.VMEM)
    return pl.pallas_call(
        row_sum_kernel,
        name="row_sum",
        grid_spec=pltpu.PrefetchScalarGridSpec(
            num_scalar_prefetch=1, grid=(), in_specs=[vmem] * 2, out_specs=[vmem] * 4
        ),
        out_shape=[jax.ShapeDtypeStruct(kept.shape[1:], jnp.float32)]
        + [jax.ShapeDtypeStruct(kept.shape[1:], jnp.bfloat16)] * 3,
        compiler_params=pltpu.CompilerParams(vmem_limit_bytes=4 << 20),
    )(z.reshape(1), kept, got)


NN = (((1,), (0,)), ((), ()))
NT = (((1,), (1,)), ((), ()))
TN = (((0,), (0,)), ((), ()))


def dot(left, right, dims):
    return lax.dot_general(left, right, dims, preferred_element_type=jnp.float32)


def halves(values):
    high = values.astype(jnp.bfloat16)
    return high, (values - high.astype(jnp.float32)).astype(jnp.bfloat16)


def dot_fine(left, right, dims):
    return dot(
        jnp.concatenate([left[0], left[0], left[1]], axis=1),
        jnp.concatenate([right[0], right[1], right[0]], axis=1),
        dims,
    )


def row_mean(values):
    return jnp.mean(values, axis=1, keepdims=True)


def row_total(values):
    return jnp.sum(values, axis=1, keepdims=True)


def attention_kernel(
    which_ref, kept_ref, near_ref, mid_ref, far_ref, first_ref, second_ref, out_ref, grad_ref
):
    f32, bf16 = jnp.float32, jnp.bfloat16
    tokens = kept_ref.shape[0]
    scale = HD ** (-0.5)
    message = jnp.where(which_ref[0] == 1, first_ref[...], second_ref[...])
    joined = kept_ref[...] + near_ref[...].astype(f32) + mid_ref[...].astype(f32)
    joined = (joined + far_ref[...].astype(f32)).astype(bf16)
    cot_one = message[:tokens]
    cot_two = message[tokens : 2 * tokens]
    gains = message[2 * tokens : 2 * tokens + 16].astype(f32)
    gain_query = gains[0:1] + gains[1:2] + gains[2:3]
    gain_key = gains[3:4] + gains[4:5] + gains[5:6]
    mask = message[2 * tokens + 16 :]

    rows = lax.broadcasted_iota(jnp.int32, (tokens, 16), 0) // 64
    picks = (rows == lax.broadcasted_iota(jnp.int32, (tokens, 16), 1)).astype(f32).astype(bf16)
    columns = lax.broadcasted_iota(jnp.int32, (HD, tokens), 1) // 64
    spots = (columns == lax.broadcasted_iota(jnp.int32, (HD, tokens), 0)).astype(f32).astype(bf16)
    opened = dot(dot(picks, mask, NN).astype(bf16), spots, NN) > 0.5
    query_at = lax.broadcasted_iota(jnp.int32, (tokens, tokens), 0)
    key_at = lax.broadcasted_iota(jnp.int32, (tokens, tokens), 1)
    allowed = (query_at // 64 == key_at // 64) | opened
    first = allowed & (key_at <= query_at)
    second = allowed & (key_at < query_at)

    values = joined.astype(f32)
    inverse = lax.rsqrt(row_mean(values * values) + EPS)
    normed = values * inverse
    queries = halves(normed * gain_query)
    keys = halves(normed * gain_key)
    scores = jnp.where(first, dot_fine(queries, keys, NT) * scale, -jnp.inf)
    expo = jnp.exp(scores - jnp.max(scores, axis=1, keepdims=True))
    soft_one = expo * (1.0 / row_total(expo))
    weights_one = soft_one.astype(bf16)
    step_one = dot(weights_one, joined, NN).astype(bf16)

    step_values = step_one.astype(f32)
    inverse_two = lax.rsqrt(row_mean(step_values * step_values) + EPS)
    renormed = step_values * inverse_two
    query_two = renormed * gain_query
    own_key = renormed * gain_key
    queries_two = halves(query_two)
    scores = jnp.where(second, dot_fine(queries_two, keys, NT) * scale, -jnp.inf)
    own_score = row_total(query_two * own_key) * scale
    top = jnp.maximum(jnp.max(scores, axis=1, keepdims=True), own_score)
    expo = jnp.exp(scores - top)
    own_expo = jnp.exp(own_score - top)
    share = 1.0 / (row_total(expo) + own_expo)
    soft_two = expo * share
    own_soft = own_expo * share
    weights_two = soft_two.astype(bf16)
    step_two = dot(weights_two, joined, NN) + own_soft * step_values
    out_ref[0] = step_one
    out_ref[1] = step_two.astype(bf16)

    d_two = cot_two.astype(f32)
    d_soft = dot(cot_two, joined, NT).astype(bf16).astype(f32)
    d_joined = dot(weights_two, cot_two, TN)
    d_own = row_total(d_two * step_values)
    d_step = own_soft * d_two
    shared = row_total(soft_two * d_soft) + own_soft * d_own
    d_scores = (soft_two * (d_soft - shared) * scale).astype(bf16)
    d_own_score = own_soft * (d_own - shared) * scale
    d_query = dot(d_scores, keys[0], NN) + d_own_score * own_key
    d_keys = dot(d_scores, queries_two[0], TN)
    d_renormed = d_query * gain_query + d_own_score * query_two * gain_key
    d_step = d_step + inverse_two * (d_renormed - renormed * row_mean(d_renormed * renormed))
    d_one = (d_step.astype(bf16).astype(f32) + cot_one.astype(f32)).astype(bf16)
    d_soft = dot(d_one, joined, NT).astype(bf16).astype(f32)
    d_joined = d_joined + dot(weights_one, d_one, TN)
    d_scores = (soft_one * (d_soft - row_total(soft_one * d_soft)) * scale).astype(bf16)
    d_query = dot(d_scores, keys[0], NN)
    d_keys = d_keys + dot(d_scores, queries[0], TN)
    d_normed = d_query * gain_query + d_keys * gain_key
    d_joined = d_joined + inverse * (d_normed - normed * row_mean(d_normed * normed))
    grad_ref[...] = d_joined.T.astype(bf16)


def attention(home, kept, pieces, messages):
    tokens = kept.shape[0]
    vmem = pl.BlockSpec(memory_space=pltpu.VMEM)
    return pl.pallas_call(
        attention_kernel,
        name="attention",
        grid_spec=pltpu.PrefetchScalarGridSpec(
            num_scalar_prefetch=1, grid=(), in_specs=[vmem] * 6, out_specs=[vmem] * 2
        ),
        out_shape=[
            jax.ShapeDtypeStruct((2, tokens, HD), jnp.bfloat16),
            jax.ShapeDtypeStruct((HD, tokens), jnp.bfloat16),
        ],
        compiler_params=pltpu.CompilerParams(vmem_limit_bytes=12 << 20),
        cost_estimate=pl.CostEstimate(
            flops=24 * 2 * tokens * tokens * HD,
            bytes_accessed=16 * tokens * HD,
            transcendentals=2 * tokens * tokens,
        ),
    )(home.reshape(1), kept, *pieces, *messages)


def keep_weights_plan(hidden, fc_weight, gain_query, gain_key, block_mask, cotangent):
    me_dp = lax.axis_index("dp")
    me_z = lax.axis_index("mp")
    me_y = lax.axis_index("section") >> 1
    me_c = lax.axis_index("section") & 1
    over_x = swap("dp", 2, 1)
    over_y = swap("section", 4, 2)
    over_c = swap("section", 4, 1)
    over_z = [swap("mp", 4, bit) for bit in range(4)]
    at_home = (me_z >> 1) == me_dp
    home = at_home.astype(jnp.int32)

    def far_half(kept, got, bits):
        kept, *sent = row_sum(me_z, kept, got)
        return kept, [over_z[b](sent[b - 1]) for b in bits], sent

    def spread_z(piece, *first):
        return jnp.stack([piece] + [after(over_z[b](piece), *first) for b in (1, 2, 3)])

    hidden_other = over_x(hidden)
    sent = streamed_product(hidden, fc_weight, 1 - me_c, jnp.bfloat16)
    kept = streamed_product(hidden, fc_weight, me_c, jnp.float32)
    sent, kept = core_sum(me_y, kept, over_c(sent))
    got = over_y(sent)
    stay, go = pack(
        me_dp ^ (1 - home), after(cotangent, sent), gain_query, gain_key, block_mask
    )
    come = over_z[2](go)
    stores = load_weights(after(fc_weight, go), me_c)
    own_kept, own_pieces, sent = far_half(kept, after(got, stores[0]), (3, 2, 1))
    crossing = jnp.where(at_home, come, stay)
    late = after(hidden_other, come, *stores)
    sent = half_product(late, stores[0], jnp.bfloat16)
    kept = half_product(late, stores[1], jnp.float32)
    sent = after(sent, *own_pieces)
    sent, kept = core_sum(me_y, kept, over_c(sent))
    got = over_y(sent)
    crossed = over_x(after(crossing, sent))
    out_own, d_own = attention(home, after(own_kept, sent), own_pieces, (stay, come))
    kept, pieces, sent = far_half(kept, after(got, d_own), (2, 3, 1))
    own_part = spread_z(d_own, *sent)
    kept = after(kept, own_part)
    own_rest = over_y(own_part)
    out_other, d_other = attention(home, kept, pieces, (crossed, crossed))
    across = over_x(out_other)
    other_part = spread_z(d_other, across, own_rest)
    other_rest = over_y(other_part)
    beside = over_z[2](jnp.where(at_home, across, out_own))

    def table(flip):
        z = me_z ^ jnp.arange(4)
        heads = [
            2 * (4 * (z & 1) + 2 * (me_y ^ flip) + core) + (z >> 1) for core in (me_c, 1 - me_c)
        ]
        return jnp.concatenate(heads).astype(jnp.int32)

    rows = fc_weight.shape[0]
    fc_grad, token = grad_rows(
        table(0),
        (own_part, over_c(own_part)),
        (other_part, over_c(other_part)),
        hidden,
        hidden_other,
        rows,
    )
    other_rest, token, beside = lax.optimization_barrier((other_rest, token, beside))
    fc_grad, ttt_out = grad_rows(
        table(1),
        (own_rest, over_c(own_rest)),
        (other_rest, over_c(other_rest)),
        hidden,
        hidden_other,
        rows,
        (home, me_dp, (out_own, across, beside), token, fc_grad),
    )
    return (ttt_out, fc_grad)


def per_device(sizes, hidden, fc_weight, *rest):
    heads = fc_weight.shape[0] // HD
    if sizes == (2, 4, 4) and heads == 16 and rest[0].shape[0] == 2 * HD:
        return keep_weights_plan(hidden, fc_weight, *rest)
    return gather_weights_plan(hidden, fc_weight, *rest)


def solution(mesh):
    in_specs = (
        P("dp", ("mp", "section")),
        P("dp", ("mp", "section")),
        P(("mp", "section")),
        P(("mp", "section")),
        P("dp", None),
        P(None, "dp", ("mp", "section")),
    )
    out_specs = (P(None, "dp", ("mp", "section")), P("dp", ("mp", "section")))
    sizes = tuple(mesh.shape[name] for name in ("dp", "mp", "section"))
    return jax.shard_map(
        partial(per_device, sizes), mesh=mesh, in_specs=in_specs, out_specs=out_specs, check_vma=False
    )
```
